512 devices in a mesh: row: 32 (over x, z), col: 16 (over y, core).
Axes of the slice: x: 4, y: 8, z: 8, core: 2. Of those that a mesh axis runs over, the one named last changes fastest.
Arguments:
- vectors: float32 [65536, 2048], P('row', 'col'), may hold values from -6 to 6
- reflectors: float32 [65536, 256], P('row'), may hold values from -0.09375 to 0.09375
- panel_factor: float32 [256, 256], replicated, as said below
- station_rows: int32 [512, 4], replicated, may hold values from 0 to 65535
- station_weights: float32 [512, 4], replicated, may hold values from -3 to 3
- event_rows: int32 [8, 4], replicated, may hold values from 0 to 65535
- event_weights: float32 [8, 4], replicated, may hold values from -3 to 3
- mode_freq: float32 [2048], P('col'), may hold values from 0.05 to 1.5
- mode_damp: float32 [2048], P('col'), may hold values from 0.0001 to 0.005
Outputs:
- rotated: float32 [65536, 2048], P('row', 'col')
- seismograms: float32 [8, 512, 1024], P(None, 'row', 'col')
The draws below stay inside these ranges and needn't reach their ends.
Inputs may be any that keep to these rules, and one draw needn't show every extreme that they name: panel_factor is upper triangular with a positive diagonal.
All inputs are finite; a program needn't handle non-finite values.
Results may differ from the reference program's by a relative error of at most 0.0003.
Values sent between devices are 32-bit elements; how exact they have to be, the bound alone decides.
No kernel may reach another device: no remote copies, remote signals or barrier semaphores. Data moves between devices by JAX's collectives and lax.ppermute only.
A program may use at most 64 MiB of HBM per device.

```python
import math
import jax
import jax.numpy as jnp
from jax import lax

NMAT = 65536
NMODE = 2048
PW = 256
COMP = 512
EV = 8
TAPS = 4
NT = 1024


def draw_panel_factor(key, part):
    key_off, key_diag = jax.random.split(jax.random.fold_in(key, 17))
    upper = jax.random.normal(key_off, (PW, PW), jnp.float32) * (0.5 / PW ** 0.5)
    diag_vals = jax.random.uniform(key_diag, (PW,), jnp.float32, 1.0, 2.0)
    upper = jnp.triu(upper, 1)
    return upper + jnp.diag(diag_vals)


def set_ends(result, stream_key, least, largest):
    place = [jax.random.randint(jax.random.fold_in(stream_key, axis), (), 0, length) for axis, length in enumerate(result.shape)]
    widest = result.shape.index(max(result.shape))
    beside = place[:widest] + [(place[widest] + 1) % result.shape[widest]] + place[widest + 1:]
    return result.at[tuple(place)].set(least).at[tuple(beside)].set(largest)


def levels(own_key, shape, shards, least, high):
    gain, own = 1.0, jax.random.fold_in(own_key, 6)
    for position, blocks in shards:
        steps = jnp.exp(jax.random.uniform(jax.random.fold_in(own, position), (blocks,), jnp.float32, least / len(shards), high / len(shards)))
        gain = gain * jnp.repeat(steps, shape[position] // blocks).reshape([-1 if axis == position else 1 for axis in range(len(shape))])
    return gain


def bell_draw(key, dims, width, limit, cuts=(), kind=jnp.bfloat16):
    result = width * jax.random.normal(key, dims, jnp.float32)
    if cuts:
        result = result * levels(key, dims, cuts, -0.22, 0.18)
    return jnp.clip(result, -limit, limit).astype(kind)


def setup_inputs(seed: int = 0) -> dict:
    seeds = jax.random.split(jax.random.key(seed), 10)
    vectors = bell_draw(seeds[0], (NMAT, NMODE), 1.0, 6.0, ((0, 32), (1, 16)), jnp.float32)
    reflectors = bell_draw(seeds[1], (NMAT, PW), (4.0 / NMAT ** 0.5), 0.09375, ((0, 32),), jnp.float32)
    panel_factor = draw_panel_factor(jax.random.fold_in(seeds[9], 71), 0)
    station_rows = set_ends(jax.random.randint(seeds[3], (COMP, TAPS), 0, NMAT), jax.random.fold_in(seeds[3], 1), 0, NMAT - 1).astype(jnp.int32)
    station_weights = bell_draw(seeds[4], (COMP, TAPS), 0.5, 3.0, (), jnp.float32)
    event_rows = set_ends(jax.random.randint(seeds[5], (EV, TAPS), 0, NMAT), jax.random.fold_in(seeds[5], 1), 0, NMAT - 1).astype(jnp.int32)
    event_weights = bell_draw(seeds[6], (EV, TAPS), 0.5, 3.0, (), jnp.float32)
    mode_freq = jnp.clip(jnp.exp(math.log(1.5) - 3.4011974 * jax.random.uniform(seeds[7], (NMODE,), jnp.float32) ** levels(seeds[7], (NMODE,), ((0, 16),), -0.2, 0.2)), 0.05, 1.5)
    mode_damp = jnp.clip(jnp.exp(math.log(0.005) - 3.912023 * jax.random.uniform(seeds[8], (NMODE,), jnp.float32) ** levels(seeds[8], (NMODE,), ((0, 16),), -0.2, 0.2)), 0.0001, 0.005)
    return {"vectors": vectors, "reflectors": reflectors, "panel_factor": panel_factor, "station_rows": station_rows, "station_weights": station_weights, "event_rows": event_rows, "event_weights": event_weights, "mode_freq": mode_freq, "mode_damp": mode_damp}


def reference(vectors, reflectors, panel_factor, station_rows, station_weights, event_rows, event_weights, mode_freq, mode_damp):
    high = lax.Precision.HIGHEST
    panel = jnp.dot(reflectors.T, vectors, precision=high, preferred_element_type=jnp.float32)
    folded = jnp.dot(panel_factor, panel, precision=high, preferred_element_type=jnp.float32)
    rotated = vectors - jnp.dot(reflectors, folded, precision=high, preferred_element_type=jnp.float32)
    receivers = lax.optimization_barrier(jnp.sum(rotated[station_rows] * station_weights[:, :, None], axis=1))
    sources = lax.optimization_barrier(jnp.sum(rotated[event_rows] * event_weights[:, :, None], axis=1))
    times = jnp.arange(NT).astype(jnp.float32)
    basis = jnp.exp(-mode_damp[:, None] * times[None, :]) * jnp.cos(mode_freq[:, None] * times[None, :])
    amplitude = (sources[:, None, :] * receivers[None, :, :]).reshape(EV * COMP, NMODE)
    summed = jnp.dot(amplitude, basis, precision=high, preferred_element_type=jnp.float32)
    seismograms = summed.reshape(EV, COMP, NT) * (1.0 / math_sqrt(NMODE))
    return (rotated, seismograms)

def math_sqrt(value):
    return float(value) ** 0.5
```

```python
import jax
import jax.numpy as jnp
from jax import lax
from jax.sharding import PartitionSpec as P

NT = 1024

ROW_BITS = (1, 8, 2, 16, 4)
COL_BITS = (8, 4, 2, 1)


def rounds(bits, n):
    return [bit for bit in bits if bit < n]


def swap(x, axis, n, bit):
    return lax.ppermute(x, axis, [(i, i ^ bit) for i in range(n)])


def all_reduce(x, axis, n, bits):
    for bit in rounds(bits, n):
        x = x + swap(x, axis, n, bit)
    return x


def all_gather(xs, axis, n, bits, dim):
    me = lax.axis_index(axis)
    for bit in rounds(bits, n):
        low = (me & bit) == 0
        others = [swap(x, axis, n, bit) for x in xs]
        xs = [
            jnp.where(low, jnp.concatenate([x, o], dim), jnp.concatenate([o, x], dim))
            for x, o in zip(xs, others)
        ]
    return xs


def reduce_scatter(x, extra, axis, n, bits):
    me = lax.axis_index(axis)
    levels = n.bit_length() - 1
    blk = x.shape[0] // n
    rest = x.shape[1:]
    order = [1 << (levels - 1 - k) for k in range(levels)]
    x = x.reshape([2] * levels + [blk] + list(rest))
    width = rest[-1]
    for bit in rounds(bits, n):
        k = order.index(bit)
        lo = lax.index_in_dim(x, 0, k, keepdims=False)
        hi = lax.index_in_dim(x, 1, k, keepdims=False)
        high = (me & bit) != 0
        keep = jnp.where(high, hi, lo)
        send = jnp.where(high, lo, hi)
        packed = jnp.concatenate([send.reshape(-1, width), extra.reshape(-1, width)], 0)
        got = swap(packed, axis, n, bit)
        cut = send.size // width
        x = keep + got[:cut].reshape(send.shape)
        extra = extra + got[cut:].reshape(extra.shape)
        order.pop(k)
    return x.reshape([blk] + list(rest)), extra


def tap_sum(field, rows, weights, first, rows_here):
    local = rows - first
    inside = (local >= 0) & (local < rows_here)
    picked = jnp.take(field, jnp.clip(local, 0, rows_here - 1), axis=0)
    scaled = jnp.where(inside, weights, 0.0)
    return jnp.sum(picked * scaled[:, :, None], axis=1)


def mode_basis(freq, damp, times):
    return jnp.exp(-damp[:, None] * times[None, :]) * jnp.cos(freq[:, None] * times[None, :])


def shards(
    vectors,
    reflectors,
    panel_factor,
    station_rows,
    station_weights,
    event_rows,
    event_weights,
    mode_freq,
    mode_damp,
):
    high = lax.Precision.HIGHEST
    nrow = lax.axis_size("row")
    ncol = lax.axis_size("col")
    rows_here = vectors.shape[0]
    first = lax.axis_index("row") * rows_here
    comp_here = station_rows.shape[0] // nrow
    events = event_rows.shape[0]
    samples = NT // ncol

    freq, damp = all_gather([mode_freq, mode_damp], "col", ncol, COL_BITS, 0)
    times = (lax.axis_index("col") * samples + jnp.arange(samples)).astype(jnp.float32)
    basis = mode_basis(freq, damp, times)

    partial_panel = jnp.dot(
        reflectors.T, vectors, precision=high, preferred_element_type=jnp.float32
    )
    panel = all_reduce(partial_panel, "row", nrow, ROW_BITS)
    folded = jnp.dot(panel_factor, panel, precision=high, preferred_element_type=jnp.float32)
    rotated = vectors - jnp.dot(
        reflectors, folded, precision=high, preferred_element_type=jnp.float32
    )
    receivers, sources = reduce_scatter(
        tap_sum(rotated, station_rows, station_weights, first, rows_here),
        tap_sum(rotated, event_rows, event_weights, first, rows_here),
        "row",
        nrow,
        ROW_BITS,
    )
    receivers, sources = all_gather([receivers, sources], "col", ncol, COL_BITS, 1)
    factor = 1.0 / float(mode_freq.shape[0] * ncol) ** 0.5
    amplitude = (sources[:, None, :] * receivers[None, :, :]).reshape(events * comp_here, -1)
    series = jnp.dot(amplitude, basis, precision=high, preferred_element_type=jnp.float32)
    seismograms = series.reshape(events, comp_here, samples) * factor
    return (rotated, seismograms)


def solution(mesh):
    placed = (P("row", "col"), P("row", None), P(), P(), P(), P(), P(), P("col"), P("col"))
    return jax.shard_map(
        shards,
        mesh=mesh,
        in_specs=placed,
        out_specs=(P("row", "col"), P(None, "row", "col")),
        check_vma=False,
    )
```

```python
import jax
import jax.numpy as jnp
from jax import lax
from jax.sharding import PartitionSpec as P

NT = 1024


def tap_sum(field, rows, weights, first, rows_here):
    local = rows - first
    inside = (local >= 0) & (local < rows_here)
    picked = jnp.take(field, jnp.clip(local, 0, rows_here - 1), axis=0)
    scaled = jnp.where(inside, weights, 0.0)
    return jnp.sum(picked * scaled[:, :, None], axis=1)


def mode_basis(freq, damp, times):
    return jnp.exp(-damp[:, None] * times[None, :]) * jnp.cos(freq[:, None] * times[None, :])


def shards(
    vectors,
    reflectors,
    panel_factor,
    station_rows,
    station_weights,
    event_rows,
    event_weights,
    mode_freq,
    mode_damp,
):
    high = lax.Precision.HIGHEST
    nrow = lax.axis_size("row")
    ncol = lax.axis_size("col")
    rows_here, width = vectors.shape
    pw = reflectors.shape[1]
    first = lax.axis_index("row") * rows_here
    comps = station_rows.shape[0]
    comp_here = comps // nrow
    events = event_rows.shape[0]
    samples = NT // ncol
    col = lax.axis_index("col")

    field = jnp.concatenate([vectors, reflectors], 1)
    taps = tap_sum(
        field,
        jnp.concatenate([station_rows, event_rows], 0),
        jnp.concatenate([station_weights, event_weights], 0),
        first,
        rows_here,
    )
    vt, rt = taps[:comps, :width], taps[:comps, width:]
    st, rs = taps[comps:, :width], taps[comps:, width:]

    partial_panel = jnp.dot(
        reflectors.T, vectors, precision=high, preferred_element_type=jnp.float32
    )
    summed = jnp.concatenate([partial_panel, st, rs.reshape(-1, width)], 0)
    total_rows = summed.shape[0]
    chunk = -(-total_rows // nrow)
    summed = jnp.pad(summed, ((0, chunk * nrow - total_rows), (0, 0)))
    send = jnp.concatenate(
        [
            summed.reshape(nrow, chunk, width),
            vt.reshape(nrow, comp_here, width),
            rt.reshape(nrow, comp_here * pw // width, width),
        ],
        1,
    )
    got = lax.all_to_all(send, "row", 0, 0).sum(0)
    mine = got[:chunk]
    vt_here = got[chunk:chunk + comp_here]
    rt_here = got[chunk + comp_here:].reshape(comp_here, pw)
    whole = lax.all_to_all(jnp.broadcast_to(mine[None], (nrow, chunk, width)), "row", 0, 0)
    whole = whole.reshape(nrow * chunk, width)
    panel = whole[:pw]
    st_all = whole[pw:pw + events]
    rs_all = whole[pw + events:total_rows].reshape(events, pw)

    folded = jnp.dot(panel_factor, panel, precision=high, preferred_element_type=jnp.float32)
    rotated = vectors - jnp.dot(
        reflectors, folded, precision=high, preferred_element_type=jnp.float32
    )
    receivers = vt_here - jnp.dot(rt_here, folded, precision=high, preferred_element_type=jnp.float32)
    sources = st_all - jnp.dot(rs_all, folded, precision=high, preferred_element_type=jnp.float32)

    block = jnp.concatenate([receivers, sources, mode_freq[None], mode_damp[None]], 0)
    parts = lax.all_to_all(jnp.broadcast_to(block[None], (ncol,) + block.shape), "col", 0, 0)
    receivers = parts[:, :comp_here].transpose(1, 0, 2).reshape(comp_here, -1)
    sources = parts[:, comp_here:comp_here + events].transpose(1, 0, 2).reshape(events, -1)
    freq = parts[:, comp_here + events].reshape(-1)
    damp = parts[:, comp_here + events + 1].reshape(-1)
    times = (col * samples + jnp.arange(samples)).astype(jnp.float32)
    basis = mode_basis(freq, damp, times)

    factor = 1.0 / float(freq.shape[0]) ** 0.5
    amplitude = (sources[:, None, :] * receivers[None, :, :]).reshape(events * comp_here, -1)
    series = jnp.dot(amplitude, basis, precision=high, preferred_element_type=jnp.float32)
    seismograms = series.reshape(events, comp_here, samples) * factor
    return (rotated, seismograms)


def solution(mesh):
    placed = (P("row", "col"), P("row", None), P(), P(), P(), P(), P(), P("col"), P("col"))
    return jax.shard_map(
        shards,
        mesh=mesh,
        in_specs=placed,
        out_specs=(P("row", "col"), P(None, "row", "col")),
        check_vma=False,
    )
```

```python
import functools

import jax
import jax.numpy as jnp
from jax import lax
from jax.experimental import pallas as pl
from jax.experimental.pallas import tpu as pltpu
from jax.sharding import PartitionSpec as P

NT = 1024


def send_kernel(taps, nrow, comp_here, events, idx_ref, w_ref, panel_ref, v_ref, r_ref, send_ref):
    width = v_ref.shape[1]
    halves = r_ref.shape[1] // width
    prow = panel_ref.shape[0] // nrow
    at_rt = prow + comp_here
    at_extra = at_rt + halves * comp_here

    def tap_rows(c):
        acc_v = acc_r = None
        for t in range(taps):
            i = idx_ref[c * taps + t]
            w = w_ref[c * taps + t]
            v = w * v_ref[pl.ds(i, 1), :]
            r = w * r_ref[pl.ds(i, 1), :]
            acc_v = v if acc_v is None else acc_v + v
            acc_r = r if acc_r is None else acc_r + r
        return acc_v, acc_r

    def dest(j, carry):
        send_ref[j, pl.ds(0, prow), :] = panel_ref[pl.ds(pl.multiple_of(j * prow, prow), prow), :]
        for cc in range(comp_here):
            acc_v, acc_r = tap_rows(j * comp_here + cc)
            send_ref[j, pl.ds(prow + cc, 1), :] = acc_v
            for h in range(halves):
                send_ref[j, pl.ds(at_rt + halves * cc + h, 1), :] = acc_r[:, h * width:(h + 1) * width]
        send_ref[j, pl.ds(at_extra, 1), :] = jnp.zeros((1, width), jnp.float32)
        return carry

    lax.fori_loop(0, nrow, dest, 0)
    for e in range(events):
        acc_v, acc_r = tap_rows(nrow * comp_here + e)
        send_ref[e, pl.ds(at_extra, 1), :] = acc_v
        for h in range(halves):
            send_ref[events + halves * e + h, pl.ds(at_extra, 1), :] = acc_r[:, h * width:(h + 1) * width]


def build_send(rows, weights, first, nrow, comp_here, events, panel, vectors, reflectors):
    rows_here, width = vectors.shape
    taps = rows.shape[1]
    local = rows - first
    inside = (local >= 0) & (local < rows_here)
    idx = jnp.clip(local, 0, rows_here - 1).reshape(-1)
    w = jnp.where(inside, weights, 0.0).reshape(-1)
    halves = reflectors.shape[1] // width
    chunk = panel.shape[0] // nrow + comp_here * (1 + halves) + 1
    smem = pl.BlockSpec(memory_space=pltpu.SMEM)
    vmem = pl.BlockSpec(memory_space=pltpu.VMEM)
    return pl.pallas_call(
        functools.partial(send_kernel, taps, nrow, comp_here, events),
        out_shape=jax.ShapeDtypeStruct((nrow, chunk, width), jnp.float32),
        in_specs=[smem, smem, vmem, vmem, vmem],
        out_specs=vmem,
    )(idx, w, panel, vectors, reflectors)


def mode_basis(freq, damp, times):
    return jnp.exp(-damp[:, None] * times[None, :]) * jnp.cos(freq[:, None] * times[None, :])


def shards(
    vectors,
    reflectors,
    panel_factor,
    station_rows,
    station_weights,
    event_rows,
    event_weights,
    mode_freq,
    mode_damp,
):
    high = lax.Precision.HIGHEST
    nrow = lax.axis_size("row")
    ncol = lax.axis_size("col")
    rows_here, width = vectors.shape
    pw = reflectors.shape[1]
    first = lax.axis_index("row") * rows_here
    comps = station_rows.shape[0]
    comp_here = comps // nrow
    events = event_rows.shape[0]
    samples = NT // ncol
    col = lax.axis_index("col")

    partial_panel = jnp.dot(
        reflectors.T, vectors, precision=high, preferred_element_type=jnp.float32
    )
    send = build_send(
        jnp.concatenate([station_rows, event_rows], 0),
        jnp.concatenate([station_weights, event_weights], 0),
        first,
        nrow,
        comp_here,
        events,
        partial_panel,
        vectors,
        reflectors,
    )
    prow = pw // nrow
    got = lax.all_to_all(send, "row", 0, 0).sum(0)
    vt_here = got[prow:prow + comp_here]
    rt_here = got[prow + comp_here:-1].reshape(comp_here, pw)
    mine = jnp.concatenate([got[:prow], got[-1:]], 0)
    whole = lax.all_to_all(jnp.broadcast_to(mine[None], (nrow,) + mine.shape), "row", 0, 0)
    panel = whole[:, :prow].reshape(pw, width)
    extra = whole[:, prow]
    st_all = extra[:events]
    rs_all = extra[events:events + events * pw // width].reshape(events, pw)

    folded = jnp.dot(panel_factor, panel, precision=high, preferred_element_type=jnp.float32)
    rotated = vectors - jnp.dot(
        reflectors, folded, precision=high, preferred_element_type=jnp.float32
    )
    receivers = vt_here - jnp.dot(rt_here, folded, precision=high, preferred_element_type=jnp.float32)
    sources = st_all - jnp.dot(rs_all, folded, precision=high, preferred_element_type=jnp.float32)

    block = jnp.concatenate([receivers, sources, mode_freq[None], mode_damp[None]], 0)
    parts = lax.all_to_all(jnp.broadcast_to(block[None], (ncol,) + block.shape), "col", 0, 0)
    receivers = parts[:, :comp_here].transpose(1, 0, 2).reshape(comp_here, -1)
    sources = parts[:, comp_here:comp_here + events].transpose(1, 0, 2).reshape(events, -1)
    freq = parts[:, comp_here + events].reshape(-1)
    damp = parts[:, comp_here + events + 1].reshape(-1)
    times = (col * samples + jnp.arange(samples)).astype(jnp.float32)
    basis = mode_basis(freq, damp, times)

    factor = 1.0 / float(freq.shape[0]) ** 0.5
    amplitude = (sources[:, None, :] * receivers[None, :, :]).reshape(events * comp_here, -1)
    series = jnp.dot(amplitude, basis, precision=high, preferred_element_type=jnp.float32)
    seismograms = series.reshape(events, comp_here, samples) * factor
    return (rotated, seismograms)


def solution(mesh):
    placed = (P("row", "col"), P("row", None), P(), P(), P(), P(), P(), P("col"), P("col"))
    return jax.shard_map(
        shards,
        mesh=mesh,
        in_specs=placed,
        out_specs=(P("row", "col"), P(None, "row", "col")),
        check_vma=False,
    )
```

```python
import functools

import jax
import jax.numpy as jnp
from jax import lax
from jax.experimental import pallas as pl
from jax.experimental.pallas import tpu as pltpu
from jax.sharding import PartitionSpec as P

NT = 1024


def send_kernel(nrow, comp_here, srow_ref, sw_ref, erow_ref, ew_ref, panel_ref, v_ref, r_ref, send_ref):
    rows_here, width = v_ref.shape
    halves = r_ref.shape[1] // width
    prow = panel_ref.shape[0] // nrow
    at_rt = prow + comp_here
    at_extra = at_rt + halves * comp_here
    taps = srow_ref.shape[1]
    events = erow_ref.shape[0]
    first = lax.axis_index("row") * rows_here

    def tap_rows(rows_ref, w_ref, c):
        acc_v = acc_r = None
        for t in range(taps):
            local = rows_ref[c, t] - first
            inside = (local >= 0) & (local < rows_here)
            i = jnp.clip(local, 0, rows_here - 1)
            w = jnp.where(inside, w_ref[c, t], 0.0)
            v = w * v_ref[pl.ds(i, 1), :]
            r = w * r_ref[pl.ds(i, 1), :]
            acc_v = v if acc_v is None else acc_v + v
            acc_r = r if acc_r is None else acc_r + r
        return acc_v, acc_r

    def dest(j, carry):
        send_ref[j, pl.ds(0, prow), :] = panel_ref[pl.ds(pl.multiple_of(j * prow, prow), prow), :]
        for cc in range(comp_here):
            acc_v, acc_r = tap_rows(srow_ref, sw_ref, j * comp_here + cc)
            send_ref[j, pl.ds(prow + cc, 1), :] = acc_v
            for h in range(halves):
                send_ref[j, pl.ds(at_rt + halves * cc + h, 1), :] = acc_r[:, h * width:(h + 1) * width]
        send_ref[j, pl.ds(at_extra, 1), :] = jnp.zeros((1, width), jnp.float32)
        return carry

    lax.fori_loop(0, nrow, dest, 0)
    for e in range(events):
        acc_v, acc_r = tap_rows(erow_ref, ew_ref, e)
        send_ref[e, pl.ds(at_extra, 1), :] = acc_v
        for h in range(halves):
            send_ref[events + halves * e + h, pl.ds(at_extra, 1), :] = acc_r[:, h * width:(h + 1) * width]


def build_send(nrow, comp_here, srows, sweights, erows, eweights, panel, vectors, reflectors):
    width = vectors.shape[1]
    halves = reflectors.shape[1] // width
    chunk = panel.shape[0] // nrow + comp_here * (1 + halves) + 1
    smem = pl.BlockSpec(memory_space=pltpu.SMEM)
    vmem = pl.BlockSpec(memory_space=pltpu.VMEM)
    return pl.pallas_call(
        functools.partial(send_kernel, nrow, comp_here),
        out_shape=jax.ShapeDtypeStruct((nrow, chunk, width), jnp.float32),
        in_specs=[smem, smem, smem, smem, vmem, vmem, vmem],
        out_specs=vmem,
    )(srows, sweights, erows, eweights, panel, vectors, reflectors)


def mode_basis(freq, damp, times):
    return jnp.exp(-damp[:, None] * times[None, :]) * jnp.cos(freq[:, None] * times[None, :])


def shards(
    vectors,
    reflectors,
    panel_factor,
    station_rows,
    station_weights,
    event_rows,
    event_weights,
    mode_freq,
    mode_damp,
):
    high = lax.Precision.HIGH
    nrow = lax.axis_size("row")
    ncol = lax.axis_size("col")
    rows_here, width = vectors.shape
    pw = reflectors.shape[1]
    first = lax.axis_index("row") * rows_here
    comps = station_rows.shape[0]
    comp_here = comps // nrow
    events = event_rows.shape[0]
    samples = NT // ncol
    col = lax.axis_index("col")

    partial_panel = jnp.dot(
        reflectors.T, vectors, precision=high, preferred_element_type=jnp.float32
    )
    send = build_send(
        nrow,
        comp_here,
        station_rows,
        station_weights,
        event_rows,
        event_weights,
        partial_panel,
        vectors,
        reflectors,
    )
    prow = pw // nrow
    got = lax.all_to_all(send, "row", 0, 0).sum(0)
    vt_here = got[prow:prow + comp_here]
    rt_here = got[prow + comp_here:-1].reshape(comp_here, pw)
    mine = jnp.concatenate([got[:prow], got[-1:]], 0)
    whole = lax.all_to_all(jnp.broadcast_to(mine[None], (nrow,) + mine.shape), "row", 0, 0)
    panel = whole[:, :prow].reshape(pw, width)
    extra = whole[:, prow]
    st_all = extra[:events]
    rs_all = extra[events:events + events * pw // width].reshape(events, pw)

    folded = jnp.dot(panel_factor, panel, precision=high, preferred_element_type=jnp.float32)
    rotated = vectors - jnp.dot(
        reflectors, folded, precision=high, preferred_element_type=jnp.float32
    )
    receivers = vt_here - jnp.dot(rt_here, folded, precision=high, preferred_element_type=jnp.float32)
    sources = st_all - jnp.dot(rs_all, folded, precision=high, preferred_element_type=jnp.float32)

    block = jnp.concatenate([receivers, sources, mode_freq[None], mode_damp[None]], 0)
    parts = lax.all_to_all(jnp.broadcast_to(block[None], (ncol,) + block.shape), "col", 0, 0)
    receivers = parts[:, :comp_here].transpose(1, 0, 2).reshape(comp_here, -1)
    sources = parts[:, comp_here:comp_here + events].transpose(1, 0, 2).reshape(events, -1)
    freq = parts[:, comp_here + events].reshape(-1)
    damp = parts[:, comp_here + events + 1].reshape(-1)
    times = (col * samples + jnp.arange(samples)).astype(jnp.float32)
    basis = mode_basis(freq, damp, times)

    factor = 1.0 / float(freq.shape[0]) ** 0.5
    amplitude = (sources[:, None, :] * receivers[None, :, :]).reshape(events * comp_here, -1)
    series = jnp.dot(amplitude, basis, precision=high, preferred_element_type=jnp.float32)
    seismograms = series.reshape(events, comp_here, samples) * factor
    return (rotated, seismograms)


def solution(mesh):
    placed = (P("row", "col"), P("row", None), P(), P(), P(), P(), P(), P("col"), P("col"))
    return jax.shard_map(
        shards,
        mesh=mesh,
        in_specs=placed,
        out_specs=(P("row", "col"), P(None, "row", "col")),
        check_vma=False,
    )
```

```python
import functools

import jax
import jax.numpy as jnp
from jax import lax
from jax.experimental import pallas as pl
from jax.experimental.pallas import tpu as pltpu
from jax.sharding import PartitionSpec as P

NT = 1024


def send_kernel(nrow, comp_here, events, taps, tab_ref, v_ref, r_ref, send_ref):
    width = v_ref.shape[1]
    pw = r_ref.shape[1]
    halves = pw // width
    prow = pw // nrow
    at_rt = prow + comp_here
    at_extra = at_rt + halves * comp_here

    panel = lax.dot_general(
        r_ref[...],
        v_ref[...],
        (((0,), (0,)), ((), ())),
        precision=lax.Precision.HIGHEST,
        preferred_element_type=jnp.float32,
    )
    for j in range(nrow):
        send_ref[j, pl.ds(0, prow), :] = panel[j * prow:(j + 1) * prow]

    def tap_rows(c):
        acc_v = acc_r = None
        for t in range(taps):
            i = tab_ref[0, c * taps + t].astype(jnp.int32)
            w = tab_ref[1, c * taps + t]
            v = w * v_ref[pl.ds(i, 1), :]
            r = w * r_ref[pl.ds(i, 1), :]
            acc_v = v if acc_v is None else acc_v + v
            acc_r = r if acc_r is None else acc_r + r
        return acc_v, acc_r

    def dest(j, carry):
        for cc in range(comp_here):
            acc_v, acc_r = tap_rows(j * comp_here + cc)
            send_ref[j, pl.ds(prow + cc, 1), :] = acc_v
            for h in range(halves):
                send_ref[j, pl.ds(at_rt + halves * cc + h, 1), :] = acc_r[:, h * width:(h + 1) * width]
        send_ref[j, pl.ds(at_extra, 1), :] = jnp.zeros((1, width), jnp.float32)
        return carry

    lax.fori_loop(0, nrow, dest, 0)
    for e in range(events):
        acc_v, acc_r = tap_rows(nrow * comp_here + e)
        send_ref[e, pl.ds(at_extra, 1), :] = acc_v
        for h in range(halves):
            send_ref[events + halves * e + h, pl.ds(at_extra, 1), :] = acc_r[:, h * width:(h + 1) * width]


def build_send(nrow, comp_here, rows, weights, first, vectors, reflectors):
    rows_here, width = vectors.shape
    taps = rows.shape[1]
    events = rows.shape[0] - nrow * comp_here
    local = rows - first
    inside = (local >= 0) & (local < rows_here)
    table = jnp.stack(
        [
            jnp.clip(local, 0, rows_here - 1).astype(jnp.float32).reshape(-1),
            jnp.where(inside, weights, 0.0).reshape(-1),
        ]
    )
    halves = reflectors.shape[1] // width
    chunk = reflectors.shape[1] // nrow + comp_here * (1 + halves) + 1
    smem = pl.BlockSpec(memory_space=pltpu.SMEM)
    vmem = pl.BlockSpec(memory_space=pltpu.VMEM)
    return pl.pallas_call(
        functools.partial(send_kernel, nrow, comp_here, events, taps),
        out_shape=jax.ShapeDtypeStruct((nrow, chunk, width), jnp.float32),
        in_specs=[smem, vmem, vmem],
        out_specs=vmem,
    )(table, vectors, reflectors)


def mode_basis(freq, damp, times):
    return jnp.exp(-damp[:, None] * times[None, :]) * jnp.cos(freq[:, None] * times[None, :])


def shards(
    vectors,
    reflectors,
    panel_factor,
    station_rows,
    station_weights,
    event_rows,
    event_weights,
    mode_freq,
    mode_damp,
):
    high = lax.Precision.HIGH
    nrow = lax.axis_size("row")
    ncol = lax.axis_size("col")
    rows_here, width = vectors.shape
    pw = reflectors.shape[1]
    first = lax.axis_index("row") * rows_here
    comps = station_rows.shape[0]
    comp_here = comps // nrow
    events = event_rows.shape[0]
    samples = NT // ncol
    col = lax.axis_index("col")

    send = build_send(
        nrow,
        comp_here,
        jnp.concatenate([station_rows, event_rows], 0),
        jnp.concatenate([station_weights, event_weights], 0),
        first,
        vectors,
        reflectors,
    )
    prow = pw // nrow
    got = lax.all_to_all(send, "row", 0, 0).sum(0)
    vt_here = got[prow:prow + comp_here]
    rt_here = got[prow + comp_here:-1].reshape(comp_here, pw)
    mine = jnp.concatenate([got[:prow], got[-1:]], 0)
    whole = lax.all_to_all(jnp.broadcast_to(mine[None], (nrow,) + mine.shape), "row", 0, 0)
    panel = whole[:, :prow].reshape(pw, width)
    extra = whole[:, prow]
    st_all = extra[:events]
    rs_all = extra[events:events + events * pw // width].reshape(events, pw)

    folded = jnp.dot(panel_factor, panel, precision=high, preferred_element_type=jnp.float32)
    rotated = vectors - jnp.dot(
        reflectors, folded, precision=high, preferred_element_type=jnp.float32
    )
    receivers = vt_here - jnp.dot(rt_here, folded, precision=high, preferred_element_type=jnp.float32)
    sources = st_all - jnp.dot(rs_all, folded, precision=high, preferred_element_type=jnp.float32)

    block = jnp.concatenate([receivers, sources, mode_freq[None], mode_damp[None]], 0)
    parts = lax.all_to_all(jnp.broadcast_to(block[None], (ncol,) + block.shape), "col", 0, 0)
    receivers = parts[:, :comp_here].transpose(1, 0, 2).reshape(comp_here, -1)
    sources = parts[:, comp_here:comp_here + events].transpose(1, 0, 2).reshape(events, -1)
    freq = parts[:, comp_here + events].reshape(-1)
    damp = parts[:, comp_here + events + 1].reshape(-1)
    times = (col * samples + jnp.arange(samples)).astype(jnp.float32)
    basis = mode_basis(freq, damp, times)

    factor = 1.0 / float(freq.shape[0]) ** 0.5
    amplitude = (sources[:, None, :] * receivers[None, :, :]).reshape(events * comp_here, -1)
    series = jnp.dot(amplitude, basis, precision=high, preferred_element_type=jnp.float32)
    seismograms = series.reshape(events, comp_here, samples) * factor
    return (rotated, seismograms)


def solution(mesh):
    placed = (P("row", "col"), P("row", None), P(), P(), P(), P(), P(), P("col"), P("col"))
    return jax.shard_map(
        shards,
        mesh=mesh,
        in_specs=placed,
        out_specs=(P("row", "col"), P(None, "row", "col")),
        check_vma=False,
    )
```

```python
import functools

import jax
import jax.numpy as jnp
from jax import lax
from jax.experimental import pallas as pl
from jax.experimental.pallas import tpu as pltpu
from jax.sharding import PartitionSpec as P

NT = 1024


def send_kernel(taps, nrow, comp_here, events, tab_ref, panel_ref, v_ref, r_ref, send_ref):
    width = v_ref.shape[1]
    halves = r_ref.shape[1] // width
    prow = panel_ref.shape[0] // nrow
    at_rt = prow + comp_here
    at_extra = at_rt + halves * comp_here

    def tap_rows(c):
        acc_v = acc_r = None
        for t in range(taps):
            i = tab_ref[0, c * taps + t].astype(jnp.int32)
            w = tab_ref[1, c * taps + t]
            v = w * v_ref[pl.ds(i, 1), :]
            r = w * r_ref[pl.ds(i, 1), :]
            acc_v = v if acc_v is None else acc_v + v
            acc_r = r if acc_r is None else acc_r + r
        return acc_v, acc_r

    def dest(j, carry):
        send_ref[j, pl.ds(0, prow), :] = panel_ref[pl.ds(pl.multiple_of(j * prow, prow), prow), :]
        for cc in range(comp_here):
            acc_v, acc_r = tap_rows(j * comp_here + cc)
            send_ref[j, pl.ds(prow + cc, 1), :] = acc_v
            for h in range(halves):
                send_ref[j, pl.ds(at_rt + halves * cc + h, 1), :] = acc_r[:, h * width:(h + 1) * width]
        send_ref[j, pl.ds(at_extra, 1), :] = jnp.zeros((1, width), jnp.float32)
        return carry

    lax.fori_loop(0, nrow, dest, 0)
    for e in range(events):
        acc_v, acc_r = tap_rows(nrow * comp_here + e)
        send_ref[e, pl.ds(at_extra, 1), :] = acc_v
        for h in range(halves):
            send_ref[events + halves * e + h, pl.ds(at_extra, 1), :] = acc_r[:, h * width:(h + 1) * width]


def build_send(rows, weights, first, nrow, comp_here, events, panel, vectors, reflectors):
    rows_here, width = vectors.shape
    taps = rows.shape[1]
    local = rows - first
    inside = (local >= 0) & (local < rows_here)
    table = jnp.stack(
        [
            jnp.clip(local, 0, rows_here - 1).astype(jnp.float32).reshape(-1),
            jnp.where(inside, weights, 0.0).reshape(-1),
        ]
    )
    halves = reflectors.shape[1] // width
    chunk = panel.shape[0] // nrow + comp_here * (1 + halves) + 1
    smem = pl.BlockSpec(memory_space=pltpu.SMEM)
    vmem = pl.BlockSpec(memory_space=pltpu.VMEM)
    return pl.pallas_call(
        functools.partial(send_kernel, taps, nrow, comp_here, events),
        out_shape=jax.ShapeDtypeStruct((nrow, chunk, width), jnp.float32),
        in_specs=[smem, vmem, vmem, vmem],
        out_specs=vmem,
    )(table, panel, vectors, reflectors)


def mode_basis(freq, damp, times):
    return jnp.exp(-damp[:, None] * times[None, :]) * jnp.cos(freq[:, None] * times[None, :])


def shards(
    vectors,
    reflectors,
    panel_factor,
    station_rows,
    station_weights,
    event_rows,
    event_weights,
    mode_freq,
    mode_damp,
):
    high = lax.Precision.HIGH
    nrow = lax.axis_size("row")
    ncol = lax.axis_size("col")
    rows_here, width = vectors.shape
    pw = reflectors.shape[1]
    first = lax.axis_index("row") * rows_here
    comps = station_rows.shape[0]
    comp_here = comps // nrow
    events = event_rows.shape[0]
    samples = NT // ncol
    col = lax.axis_index("col")

    partial_panel = jnp.dot(
        reflectors.T, vectors, precision=high, preferred_element_type=jnp.float32
    )
    send = build_send(
        jnp.concatenate([station_rows, event_rows], 0),
        jnp.concatenate([station_weights, event_weights], 0),
        first,
        nrow,
        comp_here,
        events,
        partial_panel,
        vectors,
        reflectors,
    )
    prow = pw // nrow
    got = lax.all_to_all(send, "row", 0, 0).sum(0)
    vt_here = got[prow:prow + comp_here]
    rt_here = got[prow + comp_here:-1].reshape(comp_here, pw)
    mine = jnp.concatenate([got[:prow], got[-1:]], 0)
    whole = lax.all_to_all(jnp.broadcast_to(mine[None], (nrow,) + mine.shape), "row", 0, 0)
    panel = whole[:, :prow].reshape(pw, width)
    extra = whole[:, prow]
    st_all = extra[:events]
    rs_all = extra[events:events + events * pw // width].reshape(events, pw)

    folded = jnp.dot(panel_factor, panel, precision=high, preferred_element_type=jnp.float32)
    rotated = vectors - jnp.dot(
        reflectors, folded, precision=high, preferred_element_type=jnp.float32
    )
    receivers = vt_here - jnp.dot(rt_here, folded, precision=high, preferred_element_type=jnp.float32)
    sources = st_all - jnp.dot(rs_all, folded, precision=high, preferred_element_type=jnp.float32)

    block = jnp.concatenate([receivers, sources, mode_freq[None], mode_damp[None]], 0)
    parts = lax.all_to_all(jnp.broadcast_to(block[None], (ncol,) + block.shape), "col", 0, 0)
    receivers = parts[:, :comp_here].transpose(1, 0, 2).reshape(comp_here, -1)
    sources = parts[:, comp_here:comp_here + events].transpose(1, 0, 2).reshape(events, -1)
    freq = parts[:, comp_here + events].reshape(-1)
    damp = parts[:, comp_here + events + 1].reshape(-1)
    times = (col * samples + jnp.arange(samples)).astype(jnp.float32)
    basis = mode_basis(freq, damp, times)

    factor = 1.0 / float(freq.shape[0]) ** 0.5
    amplitude = (sources[:, None, :] * receivers[None, :, :]).reshape(events * comp_here, -1)
    series = jnp.dot(amplitude, basis, precision=high, preferred_element_type=jnp.float32)
    seismograms = series.reshape(events, comp_here, samples) * factor
    return (rotated, seismograms)


def solution(mesh):
    placed = (P("row", "col"), P("row", None), P(), P(), P(), P(), P(), P("col"), P("col"))
    return jax.shard_map(
        shards,
        mesh=mesh,
        in_specs=placed,
        out_specs=(P("row", "col"), P(None, "row", "col")),
        check_vma=False,
    )
```

```python
import functools

import jax
import jax.numpy as jnp
from jax import lax
from jax.experimental import pallas as pl
from jax.experimental.pallas import tpu as pltpu
from jax.sharding import PartitionSpec as P

NT = 1024


def send_kernel(taps, nrow, comp_here, events, idx_ref, w_ref, panel_ref, v_ref, r_ref, send_ref):
    width = v_ref.shape[1]
    halves = r_ref.shape[1] // width
    prow = panel_ref.shape[0] // nrow
    at_rt = prow + comp_here
    at_extra = at_rt + halves * comp_here

    def tap_rows(c):
        acc_v = acc_r = None
        for t in range(taps):
            i = idx_ref[c * taps + t]
            w = w_ref[c * taps + t]
            v = w * v_ref[pl.ds(i, 1), :]
            r = w * r_ref[pl.ds(i, 1), :]
            acc_v = v if acc_v is None else acc_v + v
            acc_r = r if acc_r is None else acc_r + r
        return acc_v, acc_r

    def dest(j, carry):
        send_ref[j, pl.ds(0, prow), :] = panel_ref[pl.ds(pl.multiple_of(j * prow, prow), prow), :]
        for cc in range(comp_here):
            acc_v, acc_r = tap_rows(j * comp_here + cc)
            send_ref[j, pl.ds(prow + cc, 1), :] = acc_v
            for h in range(halves):
                send_ref[j, pl.ds(at_rt + halves * cc + h, 1), :] = acc_r[:, h * width:(h + 1) * width]
        send_ref[j, pl.ds(at_extra, 1), :] = jnp.zeros((1, width), jnp.float32)
        return carry

    lax.fori_loop(0, nrow, dest, 0)
    for e in range(events):
        acc_v, acc_r = tap_rows(nrow * comp_here + e)
        send_ref[e, pl.ds(at_extra, 1), :] = acc_v
        for h in range(halves):
            send_ref[events + halves * e + h, pl.ds(at_extra, 1), :] = acc_r[:, h * width:(h + 1) * width]


def build_send(rows, weights, first, nrow, comp_here, events, panel, vectors, reflectors):
    rows_here, width = vectors.shape
    taps = rows.shape[1]
    local = rows - first
    inside = (local >= 0) & (local < rows_here)
    idx = jnp.clip(local, 0, rows_here - 1).reshape(-1)
    w = jnp.where(inside, weights, 0.0).reshape(-1)
    halves = reflectors.shape[1] // width
    chunk = panel.shape[0] // nrow + comp_here * (1 + halves) + 1
    smem = pl.BlockSpec(memory_space=pltpu.SMEM)
    vmem = pl.BlockSpec(memory_space=pltpu.VMEM)
    return pl.pallas_call(
        functools.partial(send_kernel, taps, nrow, comp_here, events),
        out_shape=jax.ShapeDtypeStruct((nrow, chunk, width), jnp.float32),
        in_specs=[smem, smem, vmem, vmem, vmem],
        out_specs=vmem,
    )(idx, w, panel, vectors, reflectors)


def post_kernel(nrow, comp_here, events, got_ref, whole_ref, t_ref, freq_ref, damp_ref, folded_ref, send_ref, extra_ref):
    width = got_ref.shape[1]
    pw = t_ref.shape[0]
    prow = pw // nrow
    hi = lax.Precision.HIGHEST
    panel = whole_ref[:, pl.ds(0, prow), :].reshape(pw, width)
    folded = jnp.dot(t_ref[...], panel, precision=hi, preferred_element_type=jnp.float32)
    folded_ref[...] = folded
    f_lo, f_hi = folded[:width], folded[width:]
    vt = got_ref[pl.ds(prow, comp_here), :]
    rt_lo = got_ref[pl.ds(prow + comp_here, comp_here, stride=2), :]
    rt_hi = got_ref[pl.ds(prow + comp_here + 1, comp_here, stride=2), :]
    receivers = vt - (
        jnp.dot(rt_lo, f_lo, precision=hi, preferred_element_type=jnp.float32)
        + jnp.dot(rt_hi, f_hi, precision=hi, preferred_element_type=jnp.float32)
    )
    for j in range(3 * events):
        extra_ref[pl.ds(j, 1), :] = whole_ref[j, pl.ds(prow, 1), :]
    st = extra_ref[pl.ds(0, events), :]
    rs_lo = extra_ref[pl.ds(events, events, stride=2), :]
    rs_hi = extra_ref[pl.ds(events + 1, events, stride=2), :]
    sources = st - (
        jnp.dot(rs_lo, f_lo, precision=hi, preferred_element_type=jnp.float32)
        + jnp.dot(rs_hi, f_hi, precision=hi, preferred_element_type=jnp.float32)
    )
    for k in range(send_ref.shape[0]):
        send_ref[k, pl.ds(0, comp_here), :] = receivers
        send_ref[k, pl.ds(comp_here, events), :] = sources
        send_ref[k, pl.ds(comp_here + events, 1), :] = freq_ref[...]
        send_ref[k, pl.ds(comp_here + events + 1, 1), :] = damp_ref[...]


def build_post(nrow, ncol, comp_here, events, got, whole, panel_factor, mode_freq, mode_damp):
    width = got.shape[1]
    pw = panel_factor.shape[0]
    vmem = pl.BlockSpec(memory_space=pltpu.VMEM)
    return pl.pallas_call(
        functools.partial(post_kernel, nrow, comp_here, events),
        out_shape=(
            jax.ShapeDtypeStruct((pw, width), jnp.float32),
            jax.ShapeDtypeStruct((ncol, comp_here + events + 2, width), jnp.float32),
        ),
        in_specs=[vmem] * 5,
        out_specs=(vmem, vmem),
        scratch_shapes=[pltpu.VMEM((3 * events, width), jnp.float32)],
    )(got, whole, panel_factor, mode_freq.reshape(1, -1), mode_damp.reshape(1, -1))


def mode_basis(freq, damp, times):
    return jnp.exp(-damp[:, None] * times[None, :]) * jnp.cos(freq[:, None] * times[None, :])


def shards(
    vectors,
    reflectors,
    panel_factor,
    station_rows,
    station_weights,
    event_rows,
    event_weights,
    mode_freq,
    mode_damp,
):
    high = lax.Precision.HIGH
    nrow = lax.axis_size("row")
    ncol = lax.axis_size("col")
    rows_here, width = vectors.shape
    pw = reflectors.shape[1]
    first = lax.axis_index("row") * rows_here
    comps = station_rows.shape[0]
    comp_here = comps // nrow
    events = event_rows.shape[0]
    samples = NT // ncol
    col = lax.axis_index("col")

    partial_panel = jnp.dot(
        reflectors.T, vectors, precision=high, preferred_element_type=jnp.float32
    )
    send = build_send(
        jnp.concatenate([station_rows, event_rows], 0),
        jnp.concatenate([station_weights, event_weights], 0),
        first,
        nrow,
        comp_here,
        events,
        partial_panel,
        vectors,
        reflectors,
    )
    prow = pw // nrow
    got = lax.all_to_all(send, "row", 0, 0).sum(0)
    mine = jnp.concatenate([got[:prow], got[-1:]], 0)
    whole = lax.all_to_all(jnp.broadcast_to(mine[None], (nrow,) + mine.shape), "row", 0, 0)
    folded, block = build_post(
        nrow, ncol, comp_here, events, got, whole, panel_factor, mode_freq, mode_damp
    )
    rotated = vectors - jnp.dot(
        reflectors, folded, precision=high, preferred_element_type=jnp.float32
    )
    parts = lax.all_to_all(block, "col", 0, 0)
    receivers = parts[:, :comp_here].transpose(1, 0, 2).reshape(comp_here, -1)
    sources = parts[:, comp_here:comp_here + events].transpose(1, 0, 2).reshape(events, -1)
    freq = parts[:, comp_here + events].reshape(-1)
    damp = parts[:, comp_here + events + 1].reshape(-1)
    times = (col * samples + jnp.arange(samples)).astype(jnp.float32)
    basis = mode_basis(freq, damp, times)

    factor = 1.0 / float(freq.shape[0]) ** 0.5
    amplitude = (sources[:, None, :] * receivers[None, :, :]).reshape(events * comp_here, -1)
    series = jnp.dot(amplitude, basis, precision=high, preferred_element_type=jnp.float32)
    seismograms = series.reshape(events, comp_here, samples) * factor
    return (rotated, seismograms)


def solution(mesh):
    placed = (P("row", "col"), P("row", None), P(), P(), P(), P(), P(), P("col"), P("col"))
    return jax.shard_map(
        shards,
        mesh=mesh,
        in_specs=placed,
        out_specs=(P("row", "col"), P(None, "row", "col")),
        check_vma=False,
    )
```

```python
import functools

import jax
import jax.numpy as jnp
from jax import lax
from jax.experimental import pallas as pl
from jax.experimental.pallas import tpu as pltpu
from jax.sharding import PartitionSpec as P

NT = 1024


def tap_kernel(taps, nrow, comp_here, events, idx_ref, w_ref, rot_ref, send_ref):
    def tap_row(c):
        acc = None
        for t in range(taps):
            i = idx_ref[c * taps + t]
            w = w_ref[c * taps + t]
            v = w * rot_ref[pl.ds(i, 1), :]
            acc = v if acc is None else acc + v
        return acc

    ev = [tap_row(nrow * comp_here + e) for e in range(events)]

    def dest(j, carry):
        for cc in range(comp_here):
            send_ref[j, pl.ds(cc, 1), :] = tap_row(j * comp_here + cc)
        for e in range(events):
            send_ref[j, pl.ds(comp_here + e, 1), :] = ev[e]
        return carry

    lax.fori_loop(0, nrow, dest, 0)


def build_taps(rows, weights, first, nrow, comp_here, events, rotated):
    rows_here, width = rotated.shape
    taps = rows.shape[1]
    local = rows - first
    inside = (local >= 0) & (local < rows_here)
    idx = jnp.clip(local, 0, rows_here - 1).reshape(-1)
    w = jnp.where(inside, weights, 0.0).reshape(-1)
    smem = pl.BlockSpec(memory_space=pltpu.SMEM)
    vmem = pl.BlockSpec(memory_space=pltpu.VMEM)
    return pl.pallas_call(
        functools.partial(tap_kernel, taps, nrow, comp_here, events),
        out_shape=jax.ShapeDtypeStruct((nrow, comp_here + events, width), jnp.float32),
        in_specs=[smem, smem, vmem],
        out_specs=vmem,
    )(idx, w, rotated)


def mode_basis(freq, damp, times):
    return jnp.exp(-damp[:, None] * times[None, :]) * jnp.cos(freq[:, None] * times[None, :])


def shards(
    vectors,
    reflectors,
    panel_factor,
    station_rows,
    station_weights,
    event_rows,
    event_weights,
    mode_freq,
    mode_damp,
):
    high = lax.Precision.HIGH
    nrow = lax.axis_size("row")
    ncol = lax.axis_size("col")
    rows_here, width = vectors.shape
    pw = reflectors.shape[1]
    first = lax.axis_index("row") * rows_here
    comps = station_rows.shape[0]
    comp_here = comps // nrow
    events = event_rows.shape[0]
    samples = NT // ncol
    col = lax.axis_index("col")

    partial_panel = jnp.dot(
        reflectors.T, vectors, precision=high, preferred_element_type=jnp.float32
    )
    prow = pw // nrow
    mine = lax.all_to_all(partial_panel.reshape(nrow, prow, width), "row", 0, 0).sum(0)
    whole = lax.all_to_all(jnp.broadcast_to(mine[None], (nrow,) + mine.shape), "row", 0, 0)
    panel = whole.reshape(pw, width)
    folded = jnp.dot(panel_factor, panel, precision=high, preferred_element_type=jnp.float32)
    rotated = vectors - jnp.dot(
        reflectors, folded, precision=high, preferred_element_type=jnp.float32
    )
    send = build_taps(
        jnp.concatenate([station_rows, event_rows], 0),
        jnp.concatenate([station_weights, event_weights], 0),
        first,
        nrow,
        comp_here,
        events,
        rotated,
    )
    got = lax.all_to_all(send, "row", 0, 0).sum(0)
    block = jnp.concatenate([got, mode_freq[None], mode_damp[None]], 0)
    parts = lax.all_to_all(jnp.broadcast_to(block[None], (ncol,) + block.shape), "col", 0, 0)
    receivers = parts[:, :comp_here].transpose(1, 0, 2).reshape(comp_here, -1)
    sources = parts[:, comp_here:comp_here + events].transpose(1, 0, 2).reshape(events, -1)
    freq = parts[:, comp_here + events].reshape(-1)
    damp = parts[:, comp_here + events + 1].reshape(-1)
    times = (col * samples + jnp.arange(samples)).astype(jnp.float32)
    basis = mode_basis(freq, damp, times)

    factor = 1.0 / float(freq.shape[0]) ** 0.5
    amplitude = (sources[:, None, :] * receivers[None, :, :]).reshape(events * comp_here, -1)
    series = jnp.dot(amplitude, basis, precision=high, preferred_element_type=jnp.float32)
    seismograms = series.reshape(events, comp_here, samples) * factor
    return (rotated, seismograms)


def solution(mesh):
    placed = (P("row", "col"), P("row", None), P(), P(), P(), P(), P(), P("col"), P("col"))
    return jax.shard_map(
        shards,
        mesh=mesh,
        in_specs=placed,
        out_specs=(P("row", "col"), P(None, "row", "col")),
        check_vma=False,
    )
```

```python
import functools

import jax
import jax.numpy as jnp
from jax import lax
from jax.experimental import pallas as pl
from jax.experimental.pallas import tpu as pltpu
from jax.sharding import PartitionSpec as P

NT = 1024


def tap_kernel(taps, comp_here, idx_ref, w_ref, v_ref, r_ref, after_ref, tv_ref, tr_ref):
    del after_ref
    blocks = tv_ref.shape[0]
    count = idx_ref.shape[0] // taps

    def tap_rows(c):
        acc_v = acc_r = None
        for t in range(taps):
            i = idx_ref[c * taps + t]
            w = w_ref[c * taps + t]
            v = w * v_ref[pl.ds(i, 1), :]
            r = w * r_ref[pl.ds(i, 1), :]
            acc_v = v if acc_v is None else acc_v + v
            acc_r = r if acc_r is None else acc_r + r
        return acc_v, acc_r

    def block(j, carry):
        for cc in range(comp_here):
            acc_v, acc_r = tap_rows(j * comp_here + cc)
            tv_ref[j, pl.ds(cc, 1), :] = acc_v
            tr_ref[j, pl.ds(cc, 1), :] = acc_r
        return carry

    lax.fori_loop(0, blocks - 1, block, 0)
    last = blocks - 1
    tv_ref[last] = jnp.zeros(tv_ref.shape[1:], jnp.float32)
    tr_ref[last] = jnp.zeros(tr_ref.shape[1:], jnp.float32)
    for e in range(count - last * comp_here):
        acc_v, acc_r = tap_rows(last * comp_here + e)
        tv_ref[last, pl.ds(e, 1), :] = acc_v
        tr_ref[last, pl.ds(e, 1), :] = acc_r


def build_taps(rows, weights, first, comp_here, vectors, reflectors, after):
    rows_here, width = vectors.shape
    pw = reflectors.shape[1]
    taps = rows.shape[1]
    blocks = -(-rows.shape[0] // comp_here)
    local = rows - first
    inside = (local >= 0) & (local < rows_here)
    idx = jnp.clip(local, 0, rows_here - 1).reshape(-1)
    w = jnp.where(inside, weights, 0.0).reshape(-1)
    smem = pl.BlockSpec(memory_space=pltpu.SMEM)
    vmem = pl.BlockSpec(memory_space=pltpu.VMEM)
    taps_n = rows.shape[0] * taps
    return pl.pallas_call(
        functools.partial(tap_kernel, taps, comp_here),
        out_shape=(
            jax.ShapeDtypeStruct((blocks, comp_here, width), jnp.float32),
            jax.ShapeDtypeStruct((blocks, comp_here, pw), jnp.float32),
        ),
        in_specs=[smem, smem, vmem, vmem, vmem],
        out_specs=(vmem, vmem),
        cost_estimate=pl.CostEstimate(
            flops=2 * taps_n * (width + pw), transcendentals=0, bytes_accessed=4 * taps_n * (width + pw)
        ),
    )(idx, w, vectors, reflectors, after)


def mode_basis(freq, damp, times):
    return jnp.exp(-damp[:, None] * times[None, :]) * jnp.cos(freq[:, None] * times[None, :])


def shards(
    vectors,
    reflectors,
    panel_factor,
    station_rows,
    station_weights,
    event_rows,
    event_weights,
    mode_freq,
    mode_damp,
):
    high = lax.Precision.HIGH
    nrow = lax.axis_size("row")
    ncol = lax.axis_size("col")
    rows_here, width = vectors.shape
    pw = reflectors.shape[1]
    first = lax.axis_index("row") * rows_here
    comps = station_rows.shape[0]
    comp_here = comps // nrow
    events = event_rows.shape[0]
    samples = NT // ncol
    col = lax.axis_index("col")

    partial_panel = jnp.dot(
        reflectors.T, vectors, precision=high, preferred_element_type=jnp.float32
    )
    prow = pw // nrow
    mine = lax.all_to_all(partial_panel.reshape(nrow, prow, width), "row", 0, 0).sum(0)
    tv, tr = build_taps(
        jnp.concatenate([station_rows, event_rows], 0),
        jnp.concatenate([station_weights, event_weights], 0),
        first,
        comp_here,
        vectors,
        reflectors,
        mine,
    )
    whole = lax.all_to_all(jnp.broadcast_to(mine[None], (nrow,) + mine.shape), "row", 0, 0)
    panel = whole.reshape(pw, width)
    folded = jnp.dot(panel_factor, panel, precision=high, preferred_element_type=jnp.float32)
    blocks = tv.shape[0]
    rot_taps = tv - jnp.dot(
        tr.reshape(-1, pw), folded, precision=high, preferred_element_type=jnp.float32
    ).reshape(blocks, comp_here, width)
    send = jnp.concatenate(
        [
            rot_taps[:nrow],
            jnp.broadcast_to(rot_taps[nrow, :events][None], (nrow, events, width)),
        ],
        1,
    )
    rotated = vectors - jnp.dot(
        reflectors, folded, precision=high, preferred_element_type=jnp.float32
    )
    got = lax.all_to_all(send, "row", 0, 0).sum(0)
    block = jnp.concatenate([got, mode_freq[None], mode_damp[None]], 0)
    parts = lax.all_to_all(jnp.broadcast_to(block[None], (ncol,) + block.shape), "col", 0, 0)
    receivers = parts[:, :comp_here].transpose(1, 0, 2).reshape(comp_here, -1)
    sources = parts[:, comp_here:comp_here + events].transpose(1, 0, 2).reshape(events, -1)
    freq = parts[:, comp_here + events].reshape(-1)
    damp = parts[:, comp_here + events + 1].reshape(-1)
    times = (col * samples + jnp.arange(samples)).astype(jnp.float32)
    basis = mode_basis(freq, damp, times)

    factor = 1.0 / float(freq.shape[0]) ** 0.5
    amplitude = (sources[:, None, :] * receivers[None, :, :]).reshape(events * comp_here, -1)
    series = jnp.dot(amplitude, basis, precision=high, preferred_element_type=jnp.float32)
    seismograms = series.reshape(events, comp_here, samples) * factor
    return (rotated, seismograms)


def solution(mesh):
    placed = (P("row", "col"), P("row", None), P(), P(), P(), P(), P(), P("col"), P("col"))
    return jax.shard_map(
        shards,
        mesh=mesh,
        in_specs=placed,
        out_specs=(P("row", "col"), P(None, "row", "col")),
        check_vma=False,
    )
```

```python
import functools

import jax
import jax.numpy as jnp
from jax import lax
from jax.experimental import pallas as pl
from jax.experimental.pallas import tpu as pltpu
from jax.sharding import PartitionSpec as P

NT = 1024


def tap_kernel(taps, comp_here, idx_ref, w_ref, v_ref, r_ref, after_ref, tv_ref, tr_ref):
    del after_ref
    blocks = tv_ref.shape[0]
    count = idx_ref.shape[0] // taps

    def tap_rows(c):
        acc_v = acc_r = None
        for t in range(taps):
            i = idx_ref[c * taps + t]
            w = w_ref[c * taps + t]
            v = w * v_ref[pl.ds(i, 1), :]
            r = w * r_ref[pl.ds(i, 1), :]
            acc_v = v if acc_v is None else acc_v + v
            acc_r = r if acc_r is None else acc_r + r
        return acc_v, acc_r

    def block(j, carry):
        for cc in range(comp_here):
            acc_v, acc_r = tap_rows(j * comp_here + cc)
            tv_ref[j, pl.ds(cc, 1), :] = acc_v
            tr_ref[j, pl.ds(cc, 1), :] = acc_r
        return carry

    lax.fori_loop(0, blocks - 1, block, 0)
    last = blocks - 1
    tv_ref[last] = jnp.zeros(tv_ref.shape[1:], jnp.float32)
    tr_ref[last] = jnp.zeros(tr_ref.shape[1:], jnp.float32)
    for e in range(count - last * comp_here):
        acc_v, acc_r = tap_rows(last * comp_here + e)
        tv_ref[last, pl.ds(e, 1), :] = acc_v
        tr_ref[last, pl.ds(e, 1), :] = acc_r


def build_taps(rows, weights, first, comp_here, vectors, reflectors, after):
    rows_here, width = vectors.shape
    pw = reflectors.shape[1]
    taps = rows.shape[1]
    blocks = -(-rows.shape[0] // comp_here)
    local = rows - first
    inside = (local >= 0) & (local < rows_here)
    idx = jnp.clip(local, 0, rows_here - 1).reshape(-1)
    w = jnp.where(inside, weights, 0.0).reshape(-1)
    smem = pl.BlockSpec(memory_space=pltpu.SMEM)
    vmem = pl.BlockSpec(memory_space=pltpu.VMEM)
    taps_n = rows.shape[0] * taps
    return pl.pallas_call(
        functools.partial(tap_kernel, taps, comp_here),
        out_shape=(
            jax.ShapeDtypeStruct((blocks, comp_here, width), jnp.float32),
            jax.ShapeDtypeStruct((blocks, comp_here, pw), jnp.float32),
        ),
        in_specs=[smem, smem, vmem, vmem, vmem],
        out_specs=(vmem, vmem),
        cost_estimate=pl.CostEstimate(
            flops=2 * taps_n * (width + pw), transcendentals=0, bytes_accessed=4 * taps_n * (width + pw)
        ),
    )(idx, w, vectors, reflectors, after)


def mode_basis(freq, damp, times):
    return jnp.exp(-damp[:, None] * times[None, :]) * jnp.cos(freq[:, None] * times[None, :])


def shards(
    vectors,
    reflectors,
    panel_factor,
    station_rows,
    station_weights,
    event_rows,
    event_weights,
    mode_freq,
    mode_damp,
):
    high = lax.Precision.HIGH
    nrow = lax.axis_size("row")
    ncol = lax.axis_size("col")
    rows_here, width = vectors.shape
    pw = reflectors.shape[1]
    first = lax.axis_index("row") * rows_here
    comps = station_rows.shape[0]
    comp_here = comps // nrow
    events = event_rows.shape[0]
    samples = NT // ncol
    col = lax.axis_index("col")

    partial_panel = jnp.dot(
        reflectors.T, vectors, precision=high, preferred_element_type=jnp.float32
    )
    prow = pw // nrow
    mine = lax.all_to_all(partial_panel.reshape(nrow, prow, width), "row", 0, 0).sum(0)
    tv, tr = build_taps(
        jnp.concatenate([station_rows, event_rows], 0),
        jnp.concatenate([station_weights, event_weights], 0),
        first,
        comp_here,
        vectors,
        reflectors,
        mine,
    )
    whole = lax.all_to_all(jnp.broadcast_to(mine[None], (nrow,) + mine.shape), "row", 0, 0)
    panel = whole.reshape(pw, width)
    folded = jnp.dot(panel_factor, panel, precision=high, preferred_element_type=jnp.float32)
    blocks = tv.shape[0]
    rot_taps = tv - jnp.dot(
        tr.reshape(-1, pw), folded, precision=high, preferred_element_type=jnp.float32
    ).reshape(blocks, comp_here, width)
    send = jnp.concatenate(
        [
            rot_taps[:nrow],
            jnp.broadcast_to(rot_taps[nrow, :events][None], (nrow, events, width)),
        ],
        1,
    )
    got = lax.all_to_all(send, "row", 0, 0).sum(0)
    held, got = lax.optimization_barrier((vectors, got))
    rotated = held - jnp.dot(
        reflectors, folded, precision=high, preferred_element_type=jnp.float32
    )
    block = jnp.concatenate([got, mode_freq[None], mode_damp[None]], 0)
    parts = lax.all_to_all(jnp.broadcast_to(block[None], (ncol,) + block.shape), "col", 0, 0)
    receivers = parts[:, :comp_here].transpose(1, 0, 2).reshape(comp_here, -1)
    sources = parts[:, comp_here:comp_here + events].transpose(1, 0, 2).reshape(events, -1)
    freq = parts[:, comp_here + events].reshape(-1)
    damp = parts[:, comp_here + events + 1].reshape(-1)
    times = (col * samples + jnp.arange(samples)).astype(jnp.float32)
    basis = mode_basis(freq, damp, times)

    factor = 1.0 / float(freq.shape[0]) ** 0.5
    amplitude = (sources[:, None, :] * receivers[None, :, :]).reshape(events * comp_here, -1)
    series = jnp.dot(amplitude, basis, precision=high, preferred_element_type=jnp.float32)
    seismograms = series.reshape(events, comp_here, samples) * factor
    return (rotated, seismograms)


def solution(mesh):
    placed = (P("row", "col"), P("row", None), P(), P(), P(), P(), P(), P("col"), P("col"))
    return jax.shard_map(
        shards,
        mesh=mesh,
        in_specs=placed,
        out_specs=(P("row", "col"), P(None, "row", "col")),
        check_vma=False,
    )
```

```python
import functools

import jax
import jax.numpy as jnp
from jax import lax
from jax.experimental import pallas as pl
from jax.experimental.pallas import tpu as pltpu
from jax.sharding import PartitionSpec as P

NT = 1024


def tap_kernel(taps, comp_here, idx_ref, w_ref, v_ref, r_ref, after_ref, tv_ref, tr_ref):
    del after_ref
    blocks = tv_ref.shape[0]
    count = idx_ref.shape[0] // taps

    def tap_rows(c):
        acc_v = acc_r = None
        for t in range(taps):
            i = idx_ref[c * taps + t]
            w = w_ref[c * taps + t]
            v = w * v_ref[pl.ds(i, 1), :]
            r = w * r_ref[pl.ds(i, 1), :]
            acc_v = v if acc_v is None else acc_v + v
            acc_r = r if acc_r is None else acc_r + r
        return acc_v, acc_r

    def block(j, carry):
        for cc in range(comp_here):
            acc_v, acc_r = tap_rows(j * comp_here + cc)
            tv_ref[j, pl.ds(cc, 1), :] = acc_v
            tr_ref[j, pl.ds(cc, 1), :] = acc_r
        return carry

    lax.fori_loop(0, blocks - 1, block, 0)
    last = blocks - 1
    tv_ref[last] = jnp.zeros(tv_ref.shape[1:], jnp.float32)
    tr_ref[last] = jnp.zeros(tr_ref.shape[1:], jnp.float32)
    for e in range(count - last * comp_here):
        acc_v, acc_r = tap_rows(last * comp_here + e)
        tv_ref[last, pl.ds(e, 1), :] = acc_v
        tr_ref[last, pl.ds(e, 1), :] = acc_r


def build_taps(rows, weights, first, comp_here, vectors, reflectors, after):
    rows_here, width = vectors.shape
    pw = reflectors.shape[1]
    taps = rows.shape[1]
    blocks = -(-rows.shape[0] // comp_here)
    local = rows - first
    inside = (local >= 0) & (local < rows_here)
    idx = jnp.clip(local, 0, rows_here - 1).reshape(-1)
    w = jnp.where(inside, weights, 0.0).reshape(-1)
    smem = pl.BlockSpec(memory_space=pltpu.SMEM)
    vmem = pl.BlockSpec(memory_space=pltpu.VMEM)
    taps_n = rows.shape[0] * taps
    return pl.pallas_call(
        functools.partial(tap_kernel, taps, comp_here),
        out_shape=(
            jax.ShapeDtypeStruct((blocks, comp_here, width), jnp.float32),
            jax.ShapeDtypeStruct((blocks, comp_here, pw), jnp.float32),
        ),
        in_specs=[smem, smem, vmem, vmem, vmem],
        out_specs=(vmem, vmem),
        cost_estimate=pl.CostEstimate(
            flops=2 * taps_n * (width + pw), transcendentals=0, bytes_accessed=4 * taps_n * (width + pw)
        ),
    )(idx, w, vectors, reflectors, after)


def post_kernel(nrow, whole_ref, t_ref, tv_ref, tr_ref, folded_ref, send_ref):
    blocks, comp_here, width = tv_ref.shape
    pw = t_ref.shape[0]
    events = send_ref.shape[1] - comp_here
    hi = lax.Precision.HIGHEST
    panel = whole_ref[...].reshape(pw, width)
    folded = jnp.dot(t_ref[...], panel, precision=hi, preferred_element_type=jnp.float32)
    folded_ref[...] = folded
    tv = tv_ref[...].reshape(blocks * comp_here, width)
    tr = tr_ref[...].reshape(blocks * comp_here, pw)
    rot = tv - jnp.dot(tr, folded, precision=hi, preferred_element_type=jnp.float32)
    ev = rot[nrow * comp_here:nrow * comp_here + events]
    for j in range(nrow):
        send_ref[j, pl.ds(0, comp_here), :] = rot[j * comp_here:(j + 1) * comp_here]
        send_ref[j, pl.ds(comp_here, events), :] = ev


def build_post(nrow, events, whole, panel_factor, tv, tr):
    _, comp_here, width = tv.shape
    pw = panel_factor.shape[0]
    vmem = pl.BlockSpec(memory_space=pltpu.VMEM)
    return pl.pallas_call(
        functools.partial(post_kernel, nrow),
        out_shape=(
            jax.ShapeDtypeStruct((pw, width), jnp.float32),
            jax.ShapeDtypeStruct((nrow, comp_here + events, width), jnp.float32),
        ),
        in_specs=[vmem] * 4,
        out_specs=(vmem, vmem),
    )(whole, panel_factor, tv, tr)


def mode_basis(freq, damp, times):
    return jnp.exp(-damp[:, None] * times[None, :]) * jnp.cos(freq[:, None] * times[None, :])


def shards(
    vectors,
    reflectors,
    panel_factor,
    station_rows,
    station_weights,
    event_rows,
    event_weights,
    mode_freq,
    mode_damp,
):
    high = lax.Precision.HIGH
    nrow = lax.axis_size("row")
    ncol = lax.axis_size("col")
    rows_here, width = vectors.shape
    pw = reflectors.shape[1]
    first = lax.axis_index("row") * rows_here
    comps = station_rows.shape[0]
    comp_here = comps // nrow
    events = event_rows.shape[0]
    samples = NT // ncol
    col = lax.axis_index("col")

    partial_panel = jnp.dot(
        reflectors.T, vectors, precision=high, preferred_element_type=jnp.float32
    )
    prow = pw // nrow
    mine = lax.all_to_all(partial_panel.reshape(nrow, prow, width), "row", 0, 0).sum(0)
    tv, tr = build_taps(
        jnp.concatenate([station_rows, event_rows], 0),
        jnp.concatenate([station_weights, event_weights], 0),
        first,
        comp_here,
        vectors,
        reflectors,
        mine,
    )
    whole = lax.all_to_all(jnp.broadcast_to(mine[None], (nrow,) + mine.shape), "row", 0, 0)
    folded, send = build_post(nrow, events, whole, panel_factor, tv, tr)
    got = lax.all_to_all(send, "row", 0, 0).sum(0)
    held, got = lax.optimization_barrier((vectors, got))
    rotated = held - jnp.dot(
        reflectors, folded, precision=high, preferred_element_type=jnp.float32
    )
    block = jnp.concatenate([got, mode_freq[None], mode_damp[None]], 0)
    parts = lax.all_to_all(jnp.broadcast_to(block[None], (ncol,) + block.shape), "col", 0, 0)
    receivers = parts[:, :comp_here].transpose(1, 0, 2).reshape(comp_here, -1)
    sources = parts[:, comp_here:comp_here + events].transpose(1, 0, 2).reshape(events, -1)
    freq = parts[:, comp_here + events].reshape(-1)
    damp = parts[:, comp_here + events + 1].reshape(-1)
    times = (col * samples + jnp.arange(samples)).astype(jnp.float32)
    basis = mode_basis(freq, damp, times)

    factor = 1.0 / float(freq.shape[0]) ** 0.5
    amplitude = (sources[:, None, :] * receivers[None, :, :]).reshape(events * comp_here, -1)
    series = jnp.dot(amplitude, basis, precision=high, preferred_element_type=jnp.float32)
    seismograms = series.reshape(events, comp_here, samples) * factor
    return (rotated, seismograms)


def solution(mesh):
    placed = (P("row", "col"), P("row", None), P(), P(), P(), P(), P(), P("col"), P("col"))
    return jax.shard_map(
        shards,
        mesh=mesh,
        in_specs=placed,
        out_specs=(P("row", "col"), P(None, "row", "col")),
        check_vma=False,
    )
```

```python
import functools

import jax
import jax.numpy as jnp
from jax import lax
from jax.experimental import pallas as pl
from jax.experimental.pallas import tpu as pltpu
from jax.sharding import PartitionSpec as P

NT = 1024


def tap_kernel(taps, nrow, comp_here, events, idx_ref, w_ref, rot_ref, send_ref):
    def tap_row(c):
        acc = None
        for t in range(taps):
            i = idx_ref[c * taps + t]
            w = w_ref[c * taps + t]
            v = w * rot_ref[pl.ds(i, 1), :]
            acc = v if acc is None else acc + v
        return acc

    ev = [tap_row(nrow * comp_here + e) for e in range(events)]

    def dest(j, carry):
        for cc in range(comp_here):
            send_ref[j, pl.ds(cc, 1), :] = tap_row(j * comp_here + cc)
        for e in range(events):
            send_ref[j, pl.ds(comp_here + e, 1), :] = ev[e]
        return carry

    lax.fori_loop(0, nrow, dest, 0)


def build_taps(rows, weights, first, nrow, comp_here, events, rotated):
    rows_here, width = rotated.shape
    taps = rows.shape[1]
    local = rows - first
    inside = (local >= 0) & (local < rows_here)
    idx = jnp.clip(local, 0, rows_here - 1).reshape(-1)
    w = jnp.where(inside, weights, 0.0).reshape(-1)
    smem = pl.BlockSpec(memory_space=pltpu.SMEM)
    vmem = pl.BlockSpec(memory_space=pltpu.VMEM)
    return pl.pallas_call(
        functools.partial(tap_kernel, taps, nrow, comp_here, events),
        out_shape=jax.ShapeDtypeStruct((nrow, comp_here + events, width), jnp.float32),
        in_specs=[smem, smem, vmem],
        out_specs=vmem,
    )(idx, w, rotated)


def mode_basis(freq, damp, times):
    return jnp.exp(-damp[:, None] * times[None, :]) * jnp.cos(freq[:, None] * times[None, :])


def shards(
    vectors,
    reflectors,
    panel_factor,
    station_rows,
    station_weights,
    event_rows,
    event_weights,
    mode_freq,
    mode_damp,
):
    high = lax.Precision.HIGH
    nrow = lax.axis_size("row")
    ncol = lax.axis_size("col")
    rows_here, width = vectors.shape
    pw = reflectors.shape[1]
    first = lax.axis_index("row") * rows_here
    comps = station_rows.shape[0]
    comp_here = comps // nrow
    events = event_rows.shape[0]
    samples = NT // ncol
    col = lax.axis_index("col")

    partial_panel = jnp.dot(
        reflectors.T, vectors, precision=high, preferred_element_type=jnp.float32
    )
    prow = pw // nrow
    mine = lax.all_to_all(partial_panel.reshape(nrow, prow, width), "row", 0, 0).sum(0)
    held, mine = lax.optimization_barrier((reflectors, mine))
    whole = lax.all_to_all(jnp.broadcast_to(mine[None], (nrow,) + mine.shape), "row", 0, 0)
    factored = jnp.dot(held, panel_factor, precision=high, preferred_element_type=jnp.float32)
    panel = whole.reshape(pw, width)
    rotated = vectors - jnp.dot(
        factored, panel, precision=high, preferred_element_type=jnp.float32
    )
    send = build_taps(
        jnp.concatenate([station_rows, event_rows], 0),
        jnp.concatenate([station_weights, event_weights], 0),
        first,
        nrow,
        comp_here,
        events,
        rotated,
    )
    got = lax.all_to_all(send, "row", 0, 0).sum(0)
    block = jnp.concatenate([got, mode_freq[None], mode_damp[None]], 0)
    parts = lax.all_to_all(jnp.broadcast_to(block[None], (ncol,) + block.shape), "col", 0, 0)
    receivers = parts[:, :comp_here].transpose(1, 0, 2).reshape(comp_here, -1)
    sources = parts[:, comp_here:comp_here + events].transpose(1, 0, 2).reshape(events, -1)
    freq = parts[:, comp_here + events].reshape(-1)
    damp = parts[:, comp_here + events + 1].reshape(-1)
    times = (col * samples + jnp.arange(samples)).astype(jnp.float32)
    basis = mode_basis(freq, damp, times)

    factor = 1.0 / float(freq.shape[0]) ** 0.5
    amplitude = (sources[:, None, :] * receivers[None, :, :]).reshape(events * comp_here, -1)
    series = jnp.dot(amplitude, basis, precision=high, preferred_element_type=jnp.float32)
    seismograms = series.reshape(events, comp_here, samples) * factor
    return (rotated, seismograms)


def solution(mesh):
    placed = (P("row", "col"), P("row", None), P(), P(), P(), P(), P(), P("col"), P("col"))
    return jax.shard_map(
        shards,
        mesh=mesh,
        in_specs=placed,
        out_specs=(P("row", "col"), P(None, "row", "col")),
        check_vma=False,
    )
```

```python
import functools

import jax
import jax.numpy as jnp
from jax import lax
from jax.experimental import pallas as pl
from jax.experimental.pallas import tpu as pltpu
from jax.sharding import PartitionSpec as P

NT = 1024


def tap_kernel(taps, nrow, comp_here, events, idx_ref, w_ref, rot_ref, send_ref):
    def tap_row(c):
        acc = None
        for t in range(taps):
            i = idx_ref[c * taps + t]
            w = w_ref[c * taps + t]
            v = w * rot_ref[pl.ds(i, 1), :]
            acc = v if acc is None else acc + v
        return acc

    ev = [tap_row(nrow * comp_here + e) for e in range(events)]

    def dest(j, carry):
        for cc in range(comp_here):
            send_ref[j, pl.ds(cc, 1), :] = tap_row(j * comp_here + cc)
        for e in range(events):
            send_ref[j, pl.ds(comp_here + e, 1), :] = ev[e]
        return carry

    lax.fori_loop(0, nrow, dest, 0)


def build_taps(rows, weights, first, nrow, comp_here, events, rotated):
    rows_here, width = rotated.shape
    taps = rows.shape[1]
    local = rows - first
    inside = (local >= 0) & (local < rows_here)
    idx = jnp.clip(local, 0, rows_here - 1).reshape(-1)
    w = jnp.where(inside, weights, 0.0).reshape(-1)
    smem = pl.BlockSpec(memory_space=pltpu.SMEM)
    vmem = pl.BlockSpec(memory_space=pltpu.VMEM)
    return pl.pallas_call(
        functools.partial(tap_kernel, taps, nrow, comp_here, events),
        out_shape=jax.ShapeDtypeStruct((nrow, comp_here + events, width), jnp.float32),
        in_specs=[smem, smem, vmem],
        out_specs=vmem,
    )(idx, w, rotated)


def panel_kernel(nrow, v_ref, r_ref, out_ref):
    v = v_ref[...]
    r = r_ref[...]
    v_hi = v.astype(jnp.bfloat16)
    v_lo = (v - v_hi.astype(jnp.float32)).astype(jnp.bfloat16)
    r_hi = r.astype(jnp.bfloat16)
    r_lo = (r - r_hi.astype(jnp.float32)).astype(jnp.bfloat16)
    dims = (((0,), (0,)), ((), ()))

    def prod(a, b):
        return lax.dot_general(a, b, dims, preferred_element_type=jnp.float32)

    p = prod(r_hi, v_hi) + (prod(r_hi, v_lo) + prod(r_lo, v_hi))
    out_ref[...] = p.reshape(out_ref.shape)


def build_panel(nrow, vectors, reflectors):
    width = vectors.shape[1]
    pw = reflectors.shape[1]
    vmem = pl.BlockSpec(memory_space=pltpu.VMEM)
    return pl.pallas_call(
        functools.partial(panel_kernel, nrow),
        out_shape=jax.ShapeDtypeStruct((nrow, pw // nrow, width), jnp.float32),
        in_specs=[vmem, vmem],
        out_specs=vmem,
    )(vectors, reflectors)


def mode_basis(freq, damp, times):
    return jnp.exp(-damp[:, None] * times[None, :]) * jnp.cos(freq[:, None] * times[None, :])


def shards(
    vectors,
    reflectors,
    panel_factor,
    station_rows,
    station_weights,
    event_rows,
    event_weights,
    mode_freq,
    mode_damp,
):
    high = lax.Precision.HIGH
    nrow = lax.axis_size("row")
    ncol = lax.axis_size("col")
    rows_here, width = vectors.shape
    pw = reflectors.shape[1]
    first = lax.axis_index("row") * rows_here
    comps = station_rows.shape[0]
    comp_here = comps // nrow
    events = event_rows.shape[0]
    samples = NT // ncol
    col = lax.axis_index("col")

    prow = pw // nrow
    mine = lax.all_to_all(build_panel(nrow, vectors, reflectors), "row", 0, 0).sum(0)
    whole = lax.all_to_all(jnp.broadcast_to(mine[None], (nrow,) + mine.shape), "row", 0, 0)
    panel = whole.reshape(pw, width)
    folded = jnp.dot(panel_factor, panel, precision=high, preferred_element_type=jnp.float32)
    rotated = vectors - jnp.dot(
        reflectors, folded, precision=high, preferred_element_type=jnp.float32
    )
    send = build_taps(
        jnp.concatenate([station_rows, event_rows], 0),
        jnp.concatenate([station_weights, event_weights], 0),
        first,
        nrow,
        comp_here,
        events,
        rotated,
    )
    got = lax.all_to_all(send, "row", 0, 0).sum(0)
    block = jnp.concatenate([got, mode_freq[None], mode_damp[None]], 0)
    parts = lax.all_to_all(jnp.broadcast_to(block[None], (ncol,) + block.shape), "col", 0, 0)
    receivers = parts[:, :comp_here].transpose(1, 0, 2).reshape(comp_here, -1)
    sources = parts[:, comp_here:comp_here + events].transpose(1, 0, 2).reshape(events, -1)
    freq = parts[:, comp_here + events].reshape(-1)
    damp = parts[:, comp_here + events + 1].reshape(-1)
    times = (col * samples + jnp.arange(samples)).astype(jnp.float32)
    basis = mode_basis(freq, damp, times)

    factor = 1.0 / float(freq.shape[0]) ** 0.5
    amplitude = (sources[:, None, :] * receivers[None, :, :]).reshape(events * comp_here, -1)
    series = jnp.dot(amplitude, basis, precision=high, preferred_element_type=jnp.float32)
    seismograms = series.reshape(events, comp_here, samples) * factor
    return (rotated, seismograms)


def solution(mesh):
    placed = (P("row", "col"), P("row", None), P(), P(), P(), P(), P(), P("col"), P("col"))
    return jax.shard_map(
        shards,
        mesh=mesh,
        in_specs=placed,
        out_specs=(P("row", "col"), P(None, "row", "col")),
        check_vma=False,
    )
```

```python
import functools

import jax
import jax.numpy as jnp
from jax import lax
from jax.experimental import pallas as pl
from jax.experimental.pallas import tpu as pltpu
from jax.sharding import PartitionSpec as P

NT = 1024


def tap_kernel(taps, nrow, comp_here, events, idx_ref, w_ref, rot_ref, send_ref):
    def tap_row(c):
        acc = None
        for t in range(taps):
            i = idx_ref[c * taps + t]
            w = w_ref[c * taps + t]
            v = w * rot_ref[pl.ds(i, 1), :]
            acc = v if acc is None else acc + v
        return acc

    ev = [tap_row(nrow * comp_here + e) for e in range(events)]

    def dest(j, carry):
        for cc in range(comp_here):
            send_ref[j, pl.ds(cc, 1), :] = tap_row(j * comp_here + cc)
        for e in range(events):
            send_ref[j, pl.ds(comp_here + e, 1), :] = ev[e]
        return carry

    lax.fori_loop(0, nrow, dest, 0)


def build_taps(rows, weights, first, nrow, comp_here, events, rotated):
    rows_here, width = rotated.shape
    taps = rows.shape[1]
    local = rows - first
    inside = (local >= 0) & (local < rows_here)
    idx = jnp.clip(local, 0, rows_here - 1).reshape(-1)
    w = jnp.where(inside, weights, 0.0).reshape(-1)
    smem = pl.BlockSpec(memory_space=pltpu.SMEM)
    vmem = pl.BlockSpec(memory_space=pltpu.VMEM)
    return pl.pallas_call(
        functools.partial(tap_kernel, taps, nrow, comp_here, events),
        out_shape=jax.ShapeDtypeStruct((nrow, comp_here + events, width), jnp.float32),
        in_specs=[smem, smem, vmem],
        out_specs=vmem,
    )(idx, w, rotated)


def mode_basis(freq, damp, times):
    return jnp.exp(-damp[:, None] * times[None, :]) * jnp.cos(freq[:, None] * times[None, :])


def shards(
    vectors,
    reflectors,
    panel_factor,
    station_rows,
    station_weights,
    event_rows,
    event_weights,
    mode_freq,
    mode_damp,
):
    high = lax.Precision.HIGH
    nrow = lax.axis_size("row")
    ncol = lax.axis_size("col")
    rows_here, width = vectors.shape
    pw = reflectors.shape[1]
    first = lax.axis_index("row") * rows_here
    comps = station_rows.shape[0]
    comp_here = comps // nrow
    events = event_rows.shape[0]
    samples = NT // ncol
    col = lax.axis_index("col")

    partial_panel = jnp.dot(
        reflectors.T, vectors, precision=high, preferred_element_type=jnp.float32
    )
    prow = pw // nrow
    mine = lax.all_to_all(partial_panel.reshape(nrow, prow, width), "row", 0, 0).sum(0)
    whole = lax.all_to_all(jnp.broadcast_to(mine[None], (nrow,) + mine.shape), "row", 0, 0)
    panel = whole.reshape(pw, width)
    folded = jnp.dot(panel_factor, panel, precision=high, preferred_element_type=jnp.float32)
    rotated = vectors - jnp.dot(
        reflectors, folded, precision=high, preferred_element_type=jnp.float32
    )
    times = (col * samples + jnp.arange(samples)).astype(jnp.float32)
    times, rotated = lax.optimization_barrier((times, rotated))
    send = build_taps(
        jnp.concatenate([station_rows, event_rows], 0),
        jnp.concatenate([station_weights, event_weights], 0),
        first,
        nrow,
        comp_here,
        events,
        rotated,
    )
    got = lax.all_to_all(send, "row", 0, 0).sum(0)
    block = jnp.concatenate([got, mode_freq[None], mode_damp[None]], 0)
    parts = lax.all_to_all(jnp.broadcast_to(block[None], (ncol,) + block.shape), "col", 0, 0)
    receivers = parts[:, :comp_here].transpose(1, 0, 2).reshape(comp_here, -1)
    sources = parts[:, comp_here:comp_here + events].transpose(1, 0, 2).reshape(events, -1)
    freq = parts[:, comp_here + events].reshape(-1)
    damp = parts[:, comp_here + events + 1].reshape(-1)
    basis = mode_basis(freq, damp, times)

    factor = 1.0 / float(freq.shape[0]) ** 0.5
    amplitude = (sources[:, None, :] * receivers[None, :, :]).reshape(events * comp_here, -1)
    series = jnp.dot(amplitude, basis, precision=high, preferred_element_type=jnp.float32)
    seismograms = series.reshape(events, comp_here, samples) * factor
    return (rotated, seismograms)


def solution(mesh):
    placed = (P("row", "col"), P("row", None), P(), P(), P(), P(), P(), P("col"), P("col"))
    return jax.shard_map(
        shards,
        mesh=mesh,
        in_specs=placed,
        out_specs=(P("row", "col"), P(None, "row", "col")),
        check_vma=False,
    )
```

```python
import functools

import jax
import jax.numpy as jnp
from jax import lax
from jax.experimental import pallas as pl
from jax.experimental.pallas import tpu as pltpu
from jax.sharding import PartitionSpec as P

NT = 1024


def tap_kernel(taps, nrow, comp_here, events, idx_ref, w_ref, rot_ref, send_ref):
    def tap_row(c):
        acc = None
        for t in range(taps):
            i = idx_ref[c * taps + t]
            w = w_ref[c * taps + t]
            v = w * rot_ref[pl.ds(i, 1), :]
            acc = v if acc is None else acc + v
        return acc

    ev = [tap_row(nrow * comp_here + e) for e in range(events)]

    def dest(j, carry):
        for cc in range(comp_here):
            send_ref[j, pl.ds(cc, 1), :] = tap_row(j * comp_here + cc)
        for e in range(events):
            send_ref[j, pl.ds(comp_here + e, 1), :] = ev[e]
        return carry

    lax.fori_loop(0, nrow, dest, 0)


def build_taps(rows, weights, first, nrow, comp_here, events, rotated):
    rows_here, width = rotated.shape
    taps = rows.shape[1]
    local = rows - first
    inside = (local >= 0) & (local < rows_here)
    idx = jnp.clip(local, 0, rows_here - 1).reshape(-1)
    w = jnp.where(inside, weights, 0.0).reshape(-1)
    smem = pl.BlockSpec(memory_space=pltpu.SMEM)
    vmem = pl.BlockSpec(memory_space=pltpu.VMEM)
    return pl.pallas_call(
        functools.partial(tap_kernel, taps, nrow, comp_here, events),
        out_shape=jax.ShapeDtypeStruct((nrow, comp_here + events, width), jnp.float32),
        in_specs=[smem, smem, vmem],
        out_specs=vmem,
    )(idx, w, rotated)


def mode_basis(freq, damp, times):
    return jnp.exp(-damp[:, None] * times[None, :]) * jnp.cos(freq[:, None] * times[None, :])


def shards(
    vectors,
    reflectors,
    panel_factor,
    station_rows,
    station_weights,
    event_rows,
    event_weights,
    mode_freq,
    mode_damp,
):
    high = lax.Precision.HIGH
    nrow = lax.axis_size("row")
    ncol = lax.axis_size("col")
    rows_here, width = vectors.shape
    pw = reflectors.shape[1]
    first = lax.axis_index("row") * rows_here
    comps = station_rows.shape[0]
    comp_here = comps // nrow
    events = event_rows.shape[0]
    samples = NT // ncol
    col = lax.axis_index("col")

    partial_panel = jnp.dot(
        reflectors.T, vectors, precision=high, preferred_element_type=jnp.float32
    )
    prow = pw // nrow
    mine = lax.all_to_all(partial_panel.reshape(nrow, prow, width), "row", 0, 0).sum(0)
    whole = lax.all_to_all(jnp.broadcast_to(mine[None], (nrow,) + mine.shape), "row", 0, 0)
    panel = whole.reshape(pw, width)
    folded = jnp.dot(panel_factor, panel, precision=high, preferred_element_type=jnp.float32)
    rotated = vectors - jnp.dot(
        reflectors, folded, precision=high, preferred_element_type=jnp.float32
    )
    send = build_taps(
        jnp.concatenate([station_rows, event_rows], 0),
        jnp.concatenate([station_weights, event_weights], 0),
        first,
        nrow,
        comp_here,
        events,
        rotated,
    )
    got = lax.all_to_all(send, "row", 0, 0).sum(0)
    block = jnp.concatenate([got, mode_freq[None], mode_damp[None]], 0)
    flat = jnp.broadcast_to(block.reshape(1, -1), (ncol, block.size))
    parts = lax.all_to_all(flat, "col", 0, 0, tiled=True).reshape((ncol,) + block.shape)
    receivers = parts[:, :comp_here].transpose(1, 0, 2).reshape(comp_here, -1)
    sources = parts[:, comp_here:comp_here + events].transpose(1, 0, 2).reshape(events, -1)
    freq = parts[:, comp_here + events].reshape(-1)
    damp = parts[:, comp_here + events + 1].reshape(-1)
    times = (col * samples + jnp.arange(samples)).astype(jnp.float32)
    basis = mode_basis(freq, damp, times)

    factor = 1.0 / float(freq.shape[0]) ** 0.5
    amplitude = (sources[:, None, :] * receivers[None, :, :]).reshape(events * comp_here, -1)
    series = jnp.dot(amplitude, basis, precision=high, preferred_element_type=jnp.float32)
    seismograms = series.reshape(events, comp_here, samples) * factor
    return (rotated, seismograms)


def solution(mesh):
    placed = (P("row", "col"), P("row", None), P(), P(), P(), P(), P(), P("col"), P("col"))
    return jax.shard_map(
        shards,
        mesh=mesh,
        in_specs=placed,
        out_specs=(P("row", "col"), P(None, "row", "col")),
        check_vma=False,
    )
```

```python
import functools

import jax
import jax.numpy as jnp
from jax import lax
from jax.experimental import pallas as pl
from jax.experimental.pallas import tpu as pltpu
from jax.sharding import PartitionSpec as P

NT = 1024


def tap_kernel(taps, nrow, comp_here, events, idx_ref, w_ref, rot_ref, send_ref, ev_ref):
    def tap_row(c):
        acc = None
        for t in range(taps):
            i = idx_ref[c * taps + t]
            w = w_ref[c * taps + t]
            v = w * rot_ref[pl.ds(i, 1), :]
            acc = v if acc is None else acc + v
        return acc

    for e in range(events):
        ev_ref[pl.ds(e, 1), :] = tap_row(nrow * comp_here + e)
    ev = ev_ref[...]

    def dest(j, carry):
        for cc in range(comp_here):
            send_ref[j, pl.ds(cc, 1), :] = tap_row(j * comp_here + cc)
        send_ref[j, pl.ds(comp_here, events), :] = ev
        return carry

    lax.fori_loop(0, nrow, dest, 0)


def build_taps(rows, weights, first, nrow, comp_here, events, rotated):
    rows_here, width = rotated.shape
    taps = rows.shape[1]
    local = rows - first
    inside = (local >= 0) & (local < rows_here)
    idx = jnp.clip(local, 0, rows_here - 1).reshape(-1)
    w = jnp.where(inside, weights, 0.0).reshape(-1)
    smem = pl.BlockSpec(memory_space=pltpu.SMEM)
    vmem = pl.BlockSpec(memory_space=pltpu.VMEM)
    return pl.pallas_call(
        functools.partial(tap_kernel, taps, nrow, comp_here, events),
        out_shape=jax.ShapeDtypeStruct((nrow, comp_here + events, width), jnp.float32),
        in_specs=[smem, smem, vmem],
        out_specs=vmem,
        scratch_shapes=[pltpu.VMEM((events, width), jnp.float32)],
    )(idx, w, rotated)


def mode_basis(freq, damp, times):
    return jnp.exp(-damp[:, None] * times[None, :]) * jnp.cos(freq[:, None] * times[None, :])


def shards(
    vectors,
    reflectors,
    panel_factor,
    station_rows,
    station_weights,
    event_rows,
    event_weights,
    mode_freq,
    mode_damp,
):
    high = lax.Precision.HIGH
    nrow = lax.axis_size("row")
    ncol = lax.axis_size("col")
    rows_here, width = vectors.shape
    pw = reflectors.shape[1]
    first = lax.axis_index("row") * rows_here
    comps = station_rows.shape[0]
    comp_here = comps // nrow
    events = event_rows.shape[0]
    samples = NT // ncol
    col = lax.axis_index("col")

    partial_panel = jnp.dot(
        reflectors.T, vectors, precision=high, preferred_element_type=jnp.float32
    )
    prow = pw // nrow
    mine = lax.all_to_all(partial_panel.reshape(nrow, prow, width), "row", 0, 0).sum(0)
    whole = lax.all_to_all(jnp.broadcast_to(mine[None], (nrow,) + mine.shape), "row", 0, 0)
    panel = whole.reshape(pw, width)
    folded = jnp.dot(panel_factor, panel, precision=high, preferred_element_type=jnp.float32)
    rotated = vectors - jnp.dot(
        reflectors, folded, precision=high, preferred_element_type=jnp.float32
    )
    send = build_taps(
        jnp.concatenate([station_rows, event_rows], 0),
        jnp.concatenate([station_weights, event_weights], 0),
        first,
        nrow,
        comp_here,
        events,
        rotated,
    )
    got = lax.all_to_all(send, "row", 0, 0).sum(0)
    block = jnp.concatenate([got, mode_freq[None], mode_damp[None]], 0)
    flat = jnp.broadcast_to(block.reshape(1, -1), (ncol, block.size))
    parts = lax.all_to_all(flat, "col", 0, 0, tiled=True).reshape((ncol,) + block.shape)
    receivers = parts[:, :comp_here].transpose(1, 0, 2).reshape(comp_here, -1)
    sources = parts[:, comp_here:comp_here + events].transpose(1, 0, 2).reshape(events, -1)
    freq = parts[:, comp_here + events].reshape(-1)
    damp = parts[:, comp_here + events + 1].reshape(-1)
    times = (col * samples + jnp.arange(samples)).astype(jnp.float32)
    basis = mode_basis(freq, damp, times)

    factor = 1.0 / float(freq.shape[0]) ** 0.5
    amplitude = (sources[:, None, :] * receivers[None, :, :]).reshape(events * comp_here, -1)
    series = jnp.dot(amplitude, basis, precision=high, preferred_element_type=jnp.float32)
    seismograms = series.reshape(events, comp_here, samples) * factor
    return (rotated, seismograms)


def solution(mesh):
    placed = (P("row", "col"), P("row", None), P(), P(), P(), P(), P(), P("col"), P("col"))
    return jax.shard_map(
        shards,
        mesh=mesh,
        in_specs=placed,
        out_specs=(P("row", "col"), P(None, "row", "col")),
        check_vma=False,
    )
```

```python
import functools

import jax
import jax.numpy as jnp
from jax import lax
from jax.experimental import pallas as pl
from jax.experimental.pallas import tpu as pltpu
from jax.sharding import PartitionSpec as P

NT = 1024


def tap_kernel(taps, nrow, comp_here, events, idx_ref, w_ref, rot_ref, send_ref, ev_ref):
    def tap_row(c):
        acc = None
        for t in range(taps):
            i = idx_ref[c * taps + t]
            w = w_ref[c * taps + t]
            v = w * rot_ref[pl.ds(i, 1), :]
            acc = v if acc is None else acc + v
        return acc

    for e in range(events):
        ev_ref[pl.ds(e, 1), :] = tap_row(nrow * comp_here + e)
    ev = ev_ref[...]

    def dest(j, carry):
        send_ref[j, pl.ds(0, comp_here), :] = jnp.concatenate(
            [tap_row(j * comp_here + cc) for cc in range(comp_here)], 0
        )
        send_ref[j, pl.ds(comp_here, events), :] = ev
        return carry

    lax.fori_loop(0, nrow, dest, 0)


def build_taps(rows, weights, first, nrow, comp_here, events, rotated):
    rows_here, width = rotated.shape
    taps = rows.shape[1]
    local = rows - first
    inside = (local >= 0) & (local < rows_here)
    idx = jnp.clip(local, 0, rows_here - 1).reshape(-1)
    w = jnp.where(inside, weights, 0.0).reshape(-1)
    smem = pl.BlockSpec(memory_space=pltpu.SMEM)
    vmem = pl.BlockSpec(memory_space=pltpu.VMEM)
    return pl.pallas_call(
        functools.partial(tap_kernel, taps, nrow, comp_here, events),
        out_shape=jax.ShapeDtypeStruct((nrow, comp_here + events, width), jnp.float32),
        in_specs=[smem, smem, vmem],
        out_specs=vmem,
        scratch_shapes=[pltpu.VMEM((events, width), jnp.float32)],
    )(idx, w, rotated)


def mode_basis(freq, damp, times):
    return jnp.exp(-damp[:, None] * times[None, :]) * jnp.cos(freq[:, None] * times[None, :])


def shards(
    vectors,
    reflectors,
    panel_factor,
    station_rows,
    station_weights,
    event_rows,
    event_weights,
    mode_freq,
    mode_damp,
):
    high = lax.Precision.HIGH
    nrow = lax.axis_size("row")
    ncol = lax.axis_size("col")
    rows_here, width = vectors.shape
    pw = reflectors.shape[1]
    first = lax.axis_index("row") * rows_here
    comps = station_rows.shape[0]
    comp_here = comps // nrow
    events = event_rows.shape[0]
    samples = NT // ncol
    col = lax.axis_index("col")

    partial_panel = jnp.dot(
        reflectors.T, vectors, precision=high, preferred_element_type=jnp.float32
    )
    prow = pw // nrow
    mine = lax.all_to_all(partial_panel.reshape(nrow, prow, width), "row", 0, 0).sum(0)
    whole = lax.all_to_all(jnp.broadcast_to(mine[None], (nrow,) + mine.shape), "row", 0, 0)
    panel = whole.reshape(pw, width)
    folded = jnp.dot(panel_factor, panel, precision=high, preferred_element_type=jnp.float32)
    rotated = vectors - jnp.dot(
        reflectors, folded, precision=high, preferred_element_type=jnp.float32
    )
    send = build_taps(
        jnp.concatenate([station_rows, event_rows], 0),
        jnp.concatenate([station_weights, event_weights], 0),
        first,
        nrow,
        comp_here,
        events,
        rotated,
    )
    got = lax.all_to_all(send, "row", 0, 0).sum(0)
    block = jnp.concatenate([got, mode_freq[None], mode_damp[None]], 0)
    flat = jnp.broadcast_to(block.reshape(1, -1), (ncol, block.size))
    parts = lax.all_to_all(flat, "col", 0, 0, tiled=True).reshape((ncol,) + block.shape)
    receivers = parts[:, :comp_here].transpose(1, 0, 2).reshape(comp_here, -1)
    sources = parts[:, comp_here:comp_here + events].transpose(1, 0, 2).reshape(events, -1)
    freq = parts[:, comp_here + events].reshape(-1)
    damp = parts[:, comp_here + events + 1].reshape(-1)
    times = (col * samples + jnp.arange(samples)).astype(jnp.float32)
    basis = mode_basis(freq, damp, times)

    factor = 1.0 / float(freq.shape[0]) ** 0.5
    amplitude = (sources[:, None, :] * receivers[None, :, :]).reshape(events * comp_here, -1)
    series = jnp.dot(amplitude, basis, precision=high, preferred_element_type=jnp.float32)
    seismograms = series.reshape(events, comp_here, samples) * factor
    return (rotated, seismograms)


def solution(mesh):
    placed = (P("row", "col"), P("row", None), P(), P(), P(), P(), P(), P("col"), P("col"))
    return jax.shard_map(
        shards,
        mesh=mesh,
        in_specs=placed,
        out_specs=(P("row", "col"), P(None, "row", "col")),
        check_vma=False,
    )
```

```python
import functools

import jax
import jax.numpy as jnp
from jax import lax
from jax.experimental import pallas as pl
from jax.experimental.pallas import tpu as pltpu
from jax.sharding import PartitionSpec as P

NT = 1024


def tap_kernel(taps, nrow, comp_here, events, idx_ref, w_ref, rot_ref, send_ref, ev_ref):
    def tap_row(c):
        terms = [w_ref[c * taps + t] * rot_ref[pl.ds(idx_ref[c * taps + t], 1), :] for t in range(taps)]
        while len(terms) > 1:
            terms = [terms[k] + terms[k + 1] for k in range(0, len(terms) - 1, 2)] + terms[len(terms) - len(terms) % 2:]
        return terms[0]

    for e in range(events):
        ev_ref[pl.ds(e, 1), :] = tap_row(nrow * comp_here + e)
    ev = ev_ref[...]

    def dest(j, carry):
        for cc in range(comp_here):
            send_ref[j, pl.ds(cc, 1), :] = tap_row(j * comp_here + cc)
        send_ref[j, pl.ds(comp_here, events), :] = ev
        return carry

    lax.fori_loop(0, nrow, dest, 0, unroll=2)


def build_taps(rows, weights, first, nrow, comp_here, events, rotated):
    rows_here, width = rotated.shape
    taps = rows.shape[1]
    local = rows - first
    inside = (local >= 0) & (local < rows_here)
    idx = jnp.clip(local, 0, rows_here - 1).reshape(-1)
    w = jnp.where(inside, weights, 0.0).reshape(-1)
    smem = pl.BlockSpec(memory_space=pltpu.SMEM)
    vmem = pl.BlockSpec(memory_space=pltpu.VMEM)
    return pl.pallas_call(
        functools.partial(tap_kernel, taps, nrow, comp_here, events),
        out_shape=jax.ShapeDtypeStruct((nrow, comp_here + events, width), jnp.float32),
        in_specs=[smem, smem, vmem],
        out_specs=vmem,
        scratch_shapes=[pltpu.VMEM((events, width), jnp.float32)],
    )(idx, w, rotated)


def mode_basis(freq, damp, times):
    return jnp.exp(-damp[:, None] * times[None, :]) * jnp.cos(freq[:, None] * times[None, :])


def shards(
    vectors,
    reflectors,
    panel_factor,
    station_rows,
    station_weights,
    event_rows,
    event_weights,
    mode_freq,
    mode_damp,
):
    high = lax.Precision.HIGH
    nrow = lax.axis_size("row")
    ncol = lax.axis_size("col")
    rows_here, width = vectors.shape
    pw = reflectors.shape[1]
    first = lax.axis_index("row") * rows_here
    comps = station_rows.shape[0]
    comp_here = comps // nrow
    events = event_rows.shape[0]
    samples = NT // ncol
    col = lax.axis_index("col")

    partial_panel = jnp.dot(
        reflectors.T, vectors, precision=high, preferred_element_type=jnp.float32
    )
    prow = pw // nrow
    mine = lax.all_to_all(partial_panel.reshape(nrow, prow, width), "row", 0, 0).sum(0)
    whole = lax.all_to_all(jnp.broadcast_to(mine[None], (nrow,) + mine.shape), "row", 0, 0)
    panel = whole.reshape(pw, width)
    folded = jnp.dot(panel_factor, panel, precision=high, preferred_element_type=jnp.float32)
    rotated = vectors - jnp.dot(
        reflectors, folded, precision=high, preferred_element_type=jnp.float32
    )
    send = build_taps(
        jnp.concatenate([station_rows, event_rows], 0),
        jnp.concatenate([station_weights, event_weights], 0),
        first,
        nrow,
        comp_here,
        events,
        rotated,
    )
    got = lax.all_to_all(send, "row", 0, 0).sum(0)
    block = jnp.concatenate([got, mode_freq[None], mode_damp[None]], 0)
    flat = jnp.broadcast_to(block.reshape(1, -1), (ncol, block.size))
    parts = lax.all_to_all(flat, "col", 0, 0, tiled=True).reshape((ncol,) + block.shape)
    receivers = parts[:, :comp_here].transpose(1, 0, 2).reshape(comp_here, -1)
    sources = parts[:, comp_here:comp_here + events].transpose(1, 0, 2).reshape(events, -1)
    freq = parts[:, comp_here + events].reshape(-1)
    damp = parts[:, comp_here + events + 1].reshape(-1)
    times = (col * samples + jnp.arange(samples)).astype(jnp.float32)
    basis = mode_basis(freq, damp, times)

    factor = 1.0 / float(freq.shape[0]) ** 0.5
    amplitude = (sources[:, None, :] * receivers[None, :, :]).reshape(events * comp_here, -1)
    series = jnp.dot(amplitude, basis, precision=high, preferred_element_type=jnp.float32)
    seismograms = series.reshape(events, comp_here, samples) * factor
    return (rotated, seismograms)


def solution(mesh):
    placed = (P("row", "col"), P("row", None), P(), P(), P(), P(), P(), P("col"), P("col"))
    return jax.shard_map(
        shards,
        mesh=mesh,
        in_specs=placed,
        out_specs=(P("row", "col"), P(None, "row", "col")),
        check_vma=False,
    )
```

```python
import functools

import jax
import jax.numpy as jnp
from jax import lax
from jax.experimental import pallas as pl
from jax.experimental.pallas import tpu as pltpu
from jax.sharding import PartitionSpec as P

NT = 1024


def tap_kernel(taps, nrow, comp_here, events, idx_ref, w_ref, rot_ref, send_ref, ev_ref):
    def tap_row(c):
        terms = [w_ref[c * taps + t] * rot_ref[pl.ds(idx_ref[c * taps + t], 1), :] for t in range(taps)]
        while len(terms) > 1:
            terms = [terms[k] + terms[k + 1] for k in range(0, len(terms) - 1, 2)] + terms[len(terms) - len(terms) % 2:]
        return terms[0]

    for e in range(events):
        ev_ref[pl.ds(e, 1), :] = tap_row(nrow * comp_here + e)
    ev = ev_ref[...]

    def dest(j, carry):
        for cc in range(comp_here):
            send_ref[j, pl.ds(cc, 1), :] = tap_row(j * comp_here + cc)
        send_ref[j, pl.ds(comp_here, events), :] = ev
        return carry

    lax.fori_loop(0, nrow, dest, 0, unroll=4)


def build_taps(rows, weights, first, nrow, comp_here, events, rotated):
    rows_here, width = rotated.shape
    taps = rows.shape[1]
    local = rows - first
    inside = (local >= 0) & (local < rows_here)
    idx = jnp.clip(local, 0, rows_here - 1).reshape(-1)
    w = jnp.where(inside, weights, 0.0).reshape(-1)
    smem = pl.BlockSpec(memory_space=pltpu.SMEM)
    vmem = pl.BlockSpec(memory_space=pltpu.VMEM)
    return pl.pallas_call(
        functools.partial(tap_kernel, taps, nrow, comp_here, events),
        out_shape=jax.ShapeDtypeStruct((nrow, comp_here + events, width), jnp.float32),
        in_specs=[smem, smem, vmem],
        out_specs=vmem,
        scratch_shapes=[pltpu.VMEM((events, width), jnp.float32)],
    )(idx, w, rotated)


def mode_basis(freq, damp, times):
    return jnp.exp(-damp[:, None] * times[None, :]) * jnp.cos(freq[:, None] * times[None, :])


def shards(
    vectors,
    reflectors,
    panel_factor,
    station_rows,
    station_weights,
    event_rows,
    event_weights,
    mode_freq,
    mode_damp,
):
    high = lax.Precision.HIGH
    nrow = lax.axis_size("row")
    ncol = lax.axis_size("col")
    rows_here, width = vectors.shape
    pw = reflectors.shape[1]
    first = lax.axis_index("row") * rows_here
    comps = station_rows.shape[0]
    comp_here = comps // nrow
    events = event_rows.shape[0]
    samples = NT // ncol
    col = lax.axis_index("col")

    partial_panel = jnp.dot(
        reflectors.T, vectors, precision=high, preferred_element_type=jnp.float32
    )
    prow = pw // nrow
    mine = lax.all_to_all(partial_panel.reshape(nrow, prow, width), "row", 0, 0).sum(0)
    whole = lax.all_to_all(jnp.broadcast_to(mine[None], (nrow,) + mine.shape), "row", 0, 0)
    panel = whole.reshape(pw, width)
    folded = jnp.dot(panel_factor, panel, precision=high, preferred_element_type=jnp.float32)
    rotated = vectors - jnp.dot(
        reflectors, folded, precision=high, preferred_element_type=jnp.float32
    )
    send = build_taps(
        jnp.concatenate([station_rows, event_rows], 0),
        jnp.concatenate([station_weights, event_weights], 0),
        first,
        nrow,
        comp_here,
        events,
        rotated,
    )
    got = lax.all_to_all(send, "row", 0, 0).sum(0)
    block = jnp.concatenate([got, mode_freq[None], mode_damp[None]], 0)
    flat = jnp.broadcast_to(block.reshape(1, -1), (ncol, block.size))
    parts = lax.all_to_all(flat, "col", 0, 0, tiled=True).reshape((ncol,) + block.shape)
    receivers = parts[:, :comp_here].transpose(1, 0, 2).reshape(comp_here, -1)
    sources = parts[:, comp_here:comp_here + events].transpose(1, 0, 2).reshape(events, -1)
    freq = parts[:, comp_here + events].reshape(-1)
    damp = parts[:, comp_here + events + 1].reshape(-1)
    times = (col * samples + jnp.arange(samples)).astype(jnp.float32)
    basis = mode_basis(freq, damp, times)

    factor = 1.0 / float(freq.shape[0]) ** 0.5
    amplitude = (sources[:, None, :] * receivers[None, :, :]).reshape(events * comp_here, -1)
    series = jnp.dot(amplitude, basis, precision=high, preferred_element_type=jnp.float32)
    seismograms = series.reshape(events, comp_here, samples) * factor
    return (rotated, seismograms)


def solution(mesh):
    placed = (P("row", "col"), P("row", None), P(), P(), P(), P(), P(), P("col"), P("col"))
    return jax.shard_map(
        shards,
        mesh=mesh,
        in_specs=placed,
        out_specs=(P("row", "col"), P(None, "row", "col")),
        check_vma=False,
    )
```
